512 devices in a mesh: seq: 128 (over x, y, z_lo), dp: 4 (over z_hi, core).
Axes of the slice: x: 4, y: 4, z: 16 (z_hi: 2, z_lo: 8; z = z_hi * 8 + z_lo), core: 2. Of those that a mesh axis runs over, the one named last changes fastest.
Arguments:
- bases: int32 [4, 16384], P('dp', 'seq'), may hold values from 0 to 3
- lengths: int32 [4, 128], P('dp', 'seq'), may hold values from 64 to 128, as said below
- cotangent: bfloat16 [4, 16384, 768], P('dp', 'seq'), may hold values from -6 to 6
- first_conv_taps: bfloat16 [3, 768, 384], P(None, 'seq'), may hold values from -0.125 to 0.125
- first_projection: bfloat16 [384, 768], P('seq'), may hold values from -0.3125 to 0.3125
- second_conv_taps: bfloat16 [3, 768, 384], P(None, 'seq'), may hold values from -0.125 to 0.125
- second_projection: bfloat16 [384, 768], P('seq'), may hold values from -0.3125 to 0.3125
- embed: float32 [4, 768], replicated, may hold values from -6 to 6
Outputs:
- saliency: float32 [4, 4, 16384], P('dp', None, 'seq')
- grad_proj: float32 [589824], P(('seq', 'dp'))
The draws below stay inside these ranges and needn't reach their ends.
Inputs may be any that keep to these rules, and one draw needn't show every extreme that they name: `lengths`: every block holds between 64 and 128 live rows; in each window one block holds exactly 128 and another exactly 64.
All inputs are finite; a program needn't handle non-finite values.
Results may differ from the reference program's by a relative error of at most 0.0042.
Values may be sent and summed in bfloat16 or wider, within the bound.
A program may use at most 64 MiB of HBM per device.

```python
import math
import jax
import jax.numpy as jnp
from jax import lax

C = 768
B = 384
CAP = 128
FIRST_DILATION = 16
SECOND_DILATION = 64
WINDOW = 16384
N_SEQ = 128
N_DP = 4


def draw_lengths(key, part):
    key_vals, key_top, key_shift = jax.random.split(key, 3)
    values = jax.random.randint(key_vals, (N_DP, N_SEQ), CAP // 2, CAP + 1)
    top_idx = jax.random.randint(key_top, (N_DP,), 0, N_SEQ)
    shift_by = jax.random.randint(key_shift, (N_DP,), 1, N_SEQ)
    low_idx = (top_idx + shift_by) % N_SEQ
    columns = jnp.arange(N_SEQ)[None, :]
    values = jnp.where(columns == top_idx[:, None], CAP, values)
    values = jnp.where(columns == low_idx[:, None], CAP // 2, values)
    return values.astype(jnp.int32)


def set_ends(result, stream_key, low, top_value):
    longest = result.shape.index(max(result.shape))
    spots = []
    for shift in (0, 1):
        where = [jax.random.randint(jax.random.fold_in(stream_key, axis), (), 0, length) for axis, length in enumerate(result.shape)]
        where[longest] = (where[longest] + shift) % result.shape[longest]
        spots.append(tuple(where))
    return result.at[spots[0]].set(low).at[spots[1]].set(top_value)


def levels(stream_key, shape, pieces, smallest, top_value):
    level = 1.0
    for dim, parts in pieces:
        steps = jax.random.uniform(jax.random.fold_in(jax.random.fold_in(stream_key, 6), dim), (parts,), jnp.float32, smallest / len(pieces), top_value / len(pieces))
        level = level * jnp.repeat(jnp.exp(steps), shape[dim] // parts).reshape((-1,) + (1,) * (len(shape) - 1 - dim))
    return level


def scatter_about(stream_key, dims, width, bound, cuts=(), kind=jnp.bfloat16):
    entries = width * jax.random.normal(stream_key, dims, jnp.float32)
    if cuts:
        entries = entries * levels(stream_key, dims, cuts, -0.22, 0.18)
    return jnp.clip(entries, -bound, bound).astype(kind)


def setup_inputs(seed: int = 0) -> dict:
    arg_keys = jax.random.split(jax.random.key(seed), 9)
    bases = set_ends(jax.random.randint(arg_keys[0], (N_DP, WINDOW), 0, 4), jax.random.fold_in(arg_keys[0], 1), 0, 3).astype(jnp.int32)
    lengths = draw_lengths(jax.random.fold_in(arg_keys[8], 71), 0)
    cotangent = scatter_about(arg_keys[2], (N_DP, WINDOW, C), 1.0, 6.0, ((0, 4), (1, 128)))
    first_conv_taps = scatter_about(arg_keys[3], (3, C, B), (3 * C) ** -0.5, 0.125, ((1, 128),))
    first_projection = scatter_about(arg_keys[4], (B, C), B ** -0.5, 0.3125, ((0, 128),))
    second_conv_taps = scatter_about(arg_keys[5], (3, C, B), (3 * C) ** -0.5, 0.125, ((1, 128),))
    second_projection = scatter_about(arg_keys[6], (B, C), B ** -0.5, 0.3125, ((0, 128),))
    embed = scatter_about(arg_keys[7], (4, C), 1.0, 6.0, (), jnp.float32)
    return dict(bases=bases, lengths=lengths, cotangent=cotangent, first_conv_taps=first_conv_taps, first_projection=first_projection, second_conv_taps=second_conv_taps, second_projection=second_projection, embed=embed)


SQRT_HALF = 0.7071067811865476
INV_SQRT_TWO_PI = 0.3989422804014327

def gelu_value(values):
    return 0.5 * values * (1.0 + lax.erf(values * SQRT_HALF))

def gelu_slope(values):
    return 0.5 * (1.0 + lax.erf(values * SQRT_HALF)) + values * jnp.exp(-0.5 * values * values) * INV_SQRT_TWO_PI

def tap_sum(values, taps, dilation):
    total_rows = values.shape[0]
    padded = jnp.pad(values, ((dilation, dilation), (0, 0)))
    summed = jnp.dot(padded[:total_rows], taps[0], preferred_element_type=jnp.float32)
    summed = summed + jnp.dot(padded[dilation:dilation + total_rows], taps[1], preferred_element_type=jnp.float32)
    summed = summed + jnp.dot(padded[2 * dilation:2 * dilation + total_rows], taps[2], preferred_element_type=jnp.float32)
    return summed

def reverse_live(values, live_count):
    return jnp.roll(jnp.flip(values, 0), live_count - values.shape[0], axis=0)

def run_pass(start_rows, cot_half, live, residual_blocks):
    stream = start_rows
    saved = []
    for conv_taps, proj_matrix, dilation in residual_blocks:
        active = gelu_value(stream).astype(jnp.bfloat16)
        before = tap_sum(active, conv_taps, dilation) * live
        middle = gelu_value(before).astype(jnp.bfloat16)
        saved.append((stream, before, middle))
        stream = stream + jnp.dot(middle, proj_matrix, preferred_element_type=jnp.float32)
    grad_rows = cot_half
    proj_grads = [None, None]
    for block_idx in (1, 0):
        conv_taps, proj_matrix, dilation = residual_blocks[block_idx]
        stream_in, before, middle = saved[block_idx]
        grad_low = grad_rows.astype(jnp.bfloat16)
        proj_grads[block_idx] = jnp.dot(middle.T, grad_low, preferred_element_type=jnp.float32)
        back_mid = jnp.dot(grad_low, proj_matrix.T, preferred_element_type=jnp.float32)
        grad_before = (back_mid * gelu_slope(before) * live).astype(jnp.bfloat16)
        back_taps = jnp.stack([conv_taps[2].T, conv_taps[1].T, conv_taps[0].T])
        grad_active = tap_sum(grad_before, back_taps, dilation)
        grad_rows = grad_rows + grad_active * gelu_slope(stream_in) * live
    return (grad_rows, proj_grads)

def reference(bases, lengths, cotangent, first_conv_taps, first_projection, second_conv_taps, second_projection, embed):
    residual_blocks = [(first_conv_taps, first_projection, FIRST_DILATION), (second_conv_taps, second_projection, SECOND_DILATION)]
    slot_ids = jnp.arange(WINDOW, dtype=jnp.int32)
    device_of = slot_ids // CAP
    row_of = slot_ids % CAP
    grad_first = jnp.zeros((B, C), jnp.float32)
    grad_second = jnp.zeros((B, C), jnp.float32)
    saliency_list = []
    for window_idx in range(N_DP):
        counts = lengths[window_idx]
        starts = (jnp.cumsum(counts) - counts).astype(jnp.int32)
        live_slot = row_of < counts[device_of]
        target = jnp.where(live_slot, starts[device_of] + row_of, WINDOW).astype(jnp.int32)
        live_count = jnp.sum(counts).astype(jnp.int32)
        packed_base = jnp.zeros((WINDOW,), jnp.int32).at[target].set(bases[window_idx], mode='drop')
        packed_cot = jnp.zeros((WINDOW, C), jnp.float32).at[target].set(cotangent[window_idx].astype(jnp.float32), mode='drop')
        live = (slot_ids < live_count).astype(jnp.float32)[:, None]
        comp_base = (3 - reverse_live(packed_base, live_count)) * (slot_ids < live_count).astype(jnp.int32)
        comp_cot = reverse_live(packed_cot, live_count) * live
        grad_fwd, grads_fwd = run_pass(embed[packed_base] * live, 0.5 * packed_cot * live, live, residual_blocks)
        grad_rev, grads_rev = run_pass(embed[comp_base] * live, 0.5 * comp_cot, live, residual_blocks)
        sal_fwd = jnp.dot(grad_fwd, embed.T, precision=lax.Precision.HIGHEST)
        sal_rev = jnp.dot(grad_rev, embed.T, precision=lax.Precision.HIGHEST)
        combined = (sal_fwd + reverse_live(sal_rev, live_count)[:, ::-1]) * live / math.sqrt(C)
        back_idx = jnp.where(live_slot, target, 0).astype(jnp.int32)
        padded_sal = combined[back_idx] * live_slot.astype(jnp.float32)[:, None]
        saliency_list.append(padded_sal.T)
        grad_first = grad_first + grads_fwd[0] + grads_rev[0]
        grad_second = grad_second + grads_fwd[1] + grads_rev[1]
    grad_proj = jnp.concatenate([grad_first.reshape(-1), grad_second.reshape(-1)]) / math.sqrt(N_DP * WINDOW)
    return (jnp.stack(saliency_list), grad_proj)
```

```python
import math

import jax
import jax.numpy as jnp
import numpy as np
from jax import lax
from jax.experimental import pallas as pl
from jax.experimental.pallas import tpu as pltpu
from jax.sharding import PartitionSpec as P

MESH = pl.DeviceIdType.MESH
F32 = jnp.float32
BF16 = jnp.bfloat16
C = 768
B = 384
CAP = 128
SQRT_HALF = 0.7071067811865476
INV_SQRT_TWO_PI = 0.3989422804014327
CORE_SUM = BF16
FIRST_SUM = BF16
FAR = 1.0e6


def shard_order():
    table = np.zeros((192, 256), np.float32)
    for row in range(192):
        piece, within = divmod(row, 48)
        if piece < 3:
            source = within // 6 * 32 + piece * 6 + within % 6
        else:
            half, rest = divmod(within, 24)
            source = rest // 3 * 32 + 18 + half * 3 + rest % 3
        table[row, source] = 1.0
    return table


def class_order():
    table = np.zeros((B, B), np.float32)
    for row in range(B):
        table[row, row % 3 * 128 + row // 3] = 1.0
    return table


def triple_codes():
    table = np.zeros((128, 128), np.float32)
    for row in range(125):
        table[row, :3] = row // 25, row // 5 % 5, row % 5
    return table


def gelu_pair(values):
    bell = 1.0 + lax.erf(values * SQRT_HALF)
    slope = 0.5 * bell + values * jnp.exp(-0.5 * values * values) * INV_SQRT_TWO_PI
    return 0.5 * values * bell, slope


def dot(left, right):
    return jnp.dot(left, right, preferred_element_type=F32)


def dot_nt(left, right):
    return lax.dot_general(left, right, (((1,), (1,)), ((), ())), preferred_element_type=F32)


def dot_tn(left, right):
    return lax.dot_general(left, right, (((0,), (0,)), ((), ())), preferred_element_type=F32)


def halves(values):
    high = values.astype(BF16)
    return high, (values - high.astype(F32)).astype(BF16)


def pick(onehot, pair):
    return dot(onehot, pair[0]) + dot(onehot, pair[1])


def ones_where(mask):
    return jnp.where(mask, 1.0, 0.0)


def iota(shape, dim):
    return lax.broadcasted_iota(jnp.int32, shape, dim)


def kernel(
    bases_ref,
    len_ref,
    cot_ref,
    conv1_ref,
    proj1_ref,
    conv2_ref,
    proj2_ref,
    embed_ref,
    order_ref,
    class_ref,
    codes_ref,
    sal_ref,
    grad_ref,
    pack32,
    shard,
    zbuf,
    weights,
    tail,
    left_rows,
    right_rows,
    enc_own,
    enc_all,
    emb_fwd,
    emb_rev,
    send0,
    recv0,
    acc0,
    part_f32,
    part_low,
    recv1,
    part2,
    recv2,
    part3,
    recv3,
    send_sem,
    recv_sem,
):
    seq = lax.axis_index("seq")
    dpi = lax.axis_index("dp")
    x, y, zl = seq // 32, seq // 8 % 4, seq % 8
    zh, core = dpi // 2, dpi % 2
    z = zh * 8 + zl
    other = 1 - core
    one = y + core * (x - y)
    two = x + core * (y - x)

    def chip(first, second):
        cx = second + core * (first - second)
        cy = first + core * (second - first)
        return ((cx * 4 + cy) * 8 + zl, dpi)

    def along_z(target):
        return ((x * 4 + y) * 8 + target % 8, target // 8 * 2 + core)

    def along_seq(offset):
        return ((seq + offset + 128) % 128, dpi)

    sibling = (seq, zh * 2 + other)

    barrier = pltpu.get_barrier_semaphore()
    partners = [sibling]
    partners += [chip((one + k) % 4, two) for k in (1, 2, 3)]
    partners += [chip(one, (two + k) % 4) for k in (1, 2, 3)]
    partners += [along_z((z + k) % 16) for k in range(1, 16)]
    partners += [along_seq(k) for k in (-3, -2, -1, 1, 2, 3)]
    for device in partners:
        pl.semaphore_signal(barrier, inc=1, device_id=device, device_id_type=MESH)

    used = {"send": 0}
    started = []

    def push(source, target, slot, device):
        copy = pltpu.make_async_remote_copy(
            src_ref=source,
            dst_ref=target,
            send_sem=send_sem.at[used["send"]],
            recv_sem=recv_sem.at[slot],
            device_id=device,
            device_id_type=MESH,
        )
        used["send"] += 1
        copy.start()
        started.append(copy)

    def arrive(target, slot):
        pltpu.make_async_remote_copy(
            src_ref=target,
            dst_ref=target,
            send_sem=send_sem.at[0],
            recv_sem=recv_sem.at[slot],
            device_id=sibling,
            device_id_type=MESH,
        ).wait_recv()

    lane = iota((1, CAP), 1)
    live_count = len_ref[...]
    code_row = jnp.where(lane < live_count, bases_ref[...] + 1, 0).astype(F32)
    enc_own[...] = jnp.broadcast_to(code_row, (8, CAP))
    own_cot = cot_ref[0]
    choose = iota((80, CAP), 1) - iota((80, CAP), 0) == live_count - 80
    tail[...] = dot(ones_where(choose).astype(BF16), own_cot).astype(BF16)
    left_rows[96:128] = jnp.zeros((32, C), BF16)
    right_rows[96:128] = jnp.zeros((32, C), BF16)
    first_core = core == 0
    for k in range(3):
        pack32[6 * k : 6 * k + 6] = jnp.where(
            first_core, conv1_ref[k].astype(F32), conv2_ref[k].astype(F32)
        )
    proj_rows = jnp.where(first_core, proj1_ref[...].astype(F32), proj2_ref[...].astype(F32))
    pack32[18:21] = proj_rows[:, :B]
    pack32[21:24] = proj_rows[:, B:]
    pack32[24:32] = jnp.zeros((8, B), F32)
    shard[...] = pack32[...].astype(BF16)
    zbuf[zl] = pack32[...].astype(BF16)
    emb_fwd[0:4] = embed_ref[...]
    emb_fwd[4:8] = jnp.zeros((4, C), F32)
    emb_rev[4:8] = jnp.zeros((4, C), F32)
    for k in range(4):
        emb_rev[k : k + 1] = embed_ref[3 - k : 4 - k]

    pl.semaphore_wait(barrier, len(partners))

    Z, D1F, D1H, D2F, D2H, SIB, HALO, ENC, R0, R1, R2, R3 = (
        0, 8, 10, 12, 20, 28, 44, 48, 54, 56, 60, 64,
    )
    z_offsets = [1, 15, 2, 14, 3, 13, 4 + 8 * core]
    for offset in z_offsets:
        push(shard, zbuf.at[zl], Z + zl, along_z((z + offset) % 16))
    for k in (1, 2, 3):
        push(enc_own, enc_all.at[k - 1], ENC + k - 1, along_seq(k))
        push(enc_own, enc_all.at[2 + k], ENC + 2 + k, along_seq(-k))
    for k in range(1, 8):
        arrive(zbuf.at[(zl + k) % 8], Z + (zl + k) % 8)
    push(tail, left_rows.at[0:80], HALO, along_seq(1))
    push(cot_ref.at[0, 0:80], right_rows.at[0:80], HALO + 1, along_seq(-1))
    push(tail.at[64:80], left_rows.at[80:96], HALO + 2, along_seq(2))
    push(cot_ref.at[0, 0:16], right_rows.at[80:96], HALO + 3, along_seq(-2))

    def block_of(owner, first, second, piece, count):
        group = first * (1 + 3 * owner) + second * (4 - 3 * owner)
        rows = pl.ds(pl.multiple_of(group * 48, 16), 48)
        return weights.at[pl.ds(4 * owner + piece, count), rows, :]

    moved = dot(order_ref[...], zbuf[...].reshape(256, B)).astype(BF16)
    own_rows = pl.ds(pl.multiple_of((x * 4 + y) * 48, 16), 48)
    for k in range(4):
        weights[4 * core + k, own_rows, :] = moved[48 * k : 48 * k + 48]

    steps = (0, 3, 1, 2)

    def line(step, turn, piece=0, count=4):
        return block_of(core, (one + steps[step]) % 4, (two + steps[turn]) % 4, piece, count)

    one_up, one_down = chip((one + 1) % 4, two), chip((one + 3) % 4, two)
    two_up, two_down = chip(one, (two + 1) % 4), chip(one, (two + 3) % 4)

    def to_sibling(step, turn):
        push(line(step, turn), line(step, turn), SIB + step * 4 + turn, sibling)

    def to_second(step):
        push(line(step, 0), line(step, 0), D2F + step * 2, two_up)
        push(line(step, 0), line(step, 0), D2F + step * 2 + 1, two_down)

    def relay_second(step):
        arrive(line(step, 1), D2F + step * 2)
        push(line(step, 1, 0, 2), line(step, 1, 0, 2), D2H + step * 2, two_up)
        to_sibling(step, 1)
        arrive(line(step, 2), D2F + step * 2 + 1)
        push(line(step, 2, 2, 2), line(step, 2, 2, 2), D2H + step * 2 + 1, two_down)
        to_sibling(step, 2)

    push(line(0, 0), line(0, 0), D1F, one_up)
    push(line(0, 0), line(0, 0), D1F + 1, one_down)
    to_second(0)
    to_sibling(0, 0)
    arrive(line(1, 0), D1F)
    push(line(1, 0, 0, 2), line(1, 0, 0, 2), D1H, one_up)
    to_second(1)
    to_sibling(1, 0)
    arrive(line(2, 0), D1F + 1)
    push(line(2, 0, 2, 2), line(2, 0, 2, 2), D1H + 1, one_down)
    to_second(2)
    to_sibling(2, 0)
    relay_second(0)
    arrive(line(3, 0, 0, 2), D1H)
    arrive(line(3, 0, 2, 2), D1H + 1)
    to_second(3)
    to_sibling(3, 0)
    for step in (1, 2, 3):
        relay_second(step)
    for step in range(4):
        arrive(line(step, 3, 0, 2), D2H + step * 2)
        arrive(line(step, 3, 2, 2), D2H + step * 2 + 1)
        to_sibling(step, 3)

    for k in range(6):
        arrive(enc_all.at[k], ENC + k)
    own_n = jnp.sum(ones_where(code_row > 0.0), axis=1, keepdims=True)
    lane_f = lane.astype(F32)
    rows_t = (iota((448, 1), 0) - 160).astype(F32)
    pieces = [(code_row, jnp.zeros((1, 1), F32))]
    left_n, right_n = [], []
    left_at, right_at = jnp.zeros((1, 1), F32), own_n
    for k in (1, 2, 3):
        there = jnp.where(seq >= k, 1.0, 0.0)
        row = enc_all[k - 1, 0:1] * there
        count = jnp.sum(ones_where(row > 0.0), axis=1, keepdims=True)
        left_at = left_at - count
        left_n.append(count)
        pieces.append((row, left_at))
        there = jnp.where(seq + k <= 127, 1.0, 0.0)
        row = enc_all[2 + k, 0:1] * there
        count = jnp.sum(ones_where(row > 0.0), axis=1, keepdims=True)
        pieces.append((row, right_at))
        right_at = right_at + count
        right_n.append(count)
    found = jnp.zeros((448, CAP), F32)
    for row, start in pieces:
        found = found + jnp.where(rows_t == lane_f + start, row, 0.0)
    code = jnp.sum(found, axis=1, keepdims=True)
    flip = jnp.where(code > 0.0, 5.0 - code, 0.0)
    triple_f = 25.0 * code[0:416] + 5.0 * code[16:432] + code[32:448]
    triple_r = 25.0 * flip[32:448] + 5.0 * flip[16:432] + flip[0:416]
    hot_f = ones_where(triple_f == lane_f).astype(BF16)
    hot_r = ones_where(triple_r == lane_f).astype(BF16)

    arrive(left_rows.at[0:80], HALO)
    arrive(right_rows.at[0:80], HALO + 1)
    arrive(left_rows.at[80:96], HALO + 2)
    arrive(right_rows.at[80:96], HALO + 3)
    t288 = (iota((288, 1), 0) - 80).astype(F32)
    own_pos = jnp.where(lane_f < own_n, lane_f, FAR)
    left_pos = jnp.where(lane_f >= 80.0 - left_n[0], lane_f - 80.0, FAR)
    left_far = jnp.where(left_n[1] > 0.0, lane_f - 96.0 - left_n[0], FAR)
    left_pos = jnp.where(lane_f < 80.0, left_pos, jnp.where(lane_f < 96.0, left_far, FAR))
    right_pos = jnp.where(lane_f < right_n[0], lane_f + own_n, FAR)
    right_far = jnp.where(right_n[1] > 0.0, lane_f - 80.0 + own_n + right_n[0], FAR)
    right_pos = jnp.where(lane_f < 80.0, right_pos, jnp.where(lane_f < 96.0, right_far, FAR))
    cot = (
        dot(ones_where(t288 == own_pos).astype(BF16), own_cot)
        + dot(ones_where(t288 == left_pos).astype(BF16), left_rows[...])
        + dot(ones_where(t288 == right_pos).astype(BF16), right_rows[...])
    )
    grad2 = 0.5 * cot
    grad2_low = grad2.astype(BF16)

    for step in range(4):
        for turn in range(4):
            theirs = block_of(
                other,
                (x + core * (y - x) + steps[step]) % 4,
                (y + core * (x - y) + steps[turn]) % 4,
                0,
                4,
            )
            arrive(theirs, SIB + step * 4 + turn)

    def projection(block):
        rows = weights[4 * block + 3].astype(F32).reshape(16, 2, 24, B)
        return [rows[:, half].reshape(B, B).astype(BF16) for half in range(2)]

    proj1 = jnp.concatenate(projection(0), axis=1)
    proj2 = jnp.concatenate(projection(1), axis=1)

    before_code, mid_code, after_code = codes_ref[:, 0:1], codes_ref[:, 1:2], codes_ref[:, 2:3]
    value0, slope0 = gelu_pair(emb_fwd[...])
    low0 = value0.astype(BF16)
    hidden1 = jnp.zeros((128, B), F32)
    for k, column in enumerate((before_code, mid_code, after_code)):
        rows = dot(low0, weights[k])
        for base in range(4):
            hidden1 = hidden1 + jnp.where(column == base + 1.0, rows[base : base + 1], 0.0)
    table_live = ones_where(mid_code > 0.0)
    hidden1 = hidden1 * table_live
    value1, slope1 = gelu_pair(hidden1)
    mid1 = value1.astype(BF16)
    slope1 = halves(slope1 * table_live)
    stream1 = jnp.zeros((128, C), F32)
    for base in range(4):
        stream1 = stream1 + jnp.where(mid_code == base + 1.0, emb_fwd[base : base + 1], 0.0)
    stream1 = stream1 + dot(mid1, proj1)
    value_x, slope_x = gelu_pair(stream1)
    low_x = (value_x * table_live).astype(BF16)
    slope_x = halves(slope_x * table_live)
    taps2 = halves(jnp.concatenate([dot(low_x, weights[4 + k]) for k in range(3)], axis=0))

    hot2 = jnp.concatenate(
        [
            jnp.concatenate([hot_f[0:288], hot_f[64:352], hot_f[128:416]], axis=1),
            jnp.concatenate([hot_r[128:416], hot_r[64:352], hot_r[0:288]], axis=1),
        ],
        axis=0,
    )
    hidden2 = pick(hot2, taps2)
    value2, slope2 = gelu_pair(hidden2)
    live288 = ones_where(code[80:368] > 0.0)
    back2 = dot_nt(grad2_low, proj2) * live288
    own_mask = ones_where(iota((CAP, 1), 0).astype(F32) < own_n)
    mid2 = jnp.concatenate([value2[80:208] * own_mask, value2[368:496] * own_mask], axis=0)
    classes = class_ref[...]
    mid2 = dot(mid2.astype(BF16), classes).astype(BF16)
    own_grad2 = grad2_low[80:208]
    sum2 = dot_tn(mid2, jnp.concatenate([own_grad2, own_grad2], axis=0))

    def to_core(block, total):
        first = jnp.concatenate([total[0:128], total[128:256, 0:B]], axis=1)
        second = jnp.concatenate([total[128:256, B:], total[256:384]], axis=1)
        send0[block] = jnp.where(first_core, second, first).astype(CORE_SUM).reshape(8, 16, 1152)
        acc0[block] = jnp.where(first_core, first, second).reshape(8, 16, 1152)
        push(send0.at[block], recv0.at[block], R0 + block, sibling)

    to_core(1, sum2)
    gh_f = (back2 * slope2[0:288]).astype(BF16)
    gh_r = (back2 * slope2[288:576]).astype(BF16)
    near2 = [
        jnp.concatenate([gh_f[128:288], gh_r[0:160]], axis=0),
        jnp.concatenate([gh_f[64:224], gh_r[64:224]], axis=0),
        jnp.concatenate([gh_f[0:160], gh_r[128:288]], axis=0),
    ]
    active2 = dot_nt(near2[0], weights[4])
    active2 = active2 + dot_nt(near2[1], weights[5])
    active2 = active2 + dot_nt(near2[2], weights[6])
    hot1 = jnp.concatenate([hot_f[128:288], hot_r[128:288]], axis=0)
    around = grad2[64:224]
    grad1 = jnp.concatenate([around, around], axis=0) + active2 * pick(hot1, slope_x)
    grad1_low = grad1.astype(BF16)

    own_low = own_mask.astype(BF16)
    own_hot = jnp.concatenate([hot_f[144:272] * own_low, hot_r[144:272] * own_low], axis=0)
    mid1 = dot(own_hot, dot(mid1, classes).astype(BF16)).astype(BF16)
    sum1 = dot_tn(mid1, jnp.concatenate([grad1_low[16:144], grad1_low[176:304]], axis=0))
    to_core(0, sum1)
    back1 = dot_nt(grad1_low, proj1)
    gh1 = (back1 * pick(hot1, slope1)).astype(BF16)
    near1 = [
        jnp.concatenate([gh1[32:160], gh1[160:288]], axis=0),
        jnp.concatenate([gh1[16:144], gh1[176:304]], axis=0),
        jnp.concatenate([gh1[0:128], gh1[192:320]], axis=0),
    ]

    for block in (1, 0):
        arrive(recv0.at[block], R0 + block)
        for piece in range(8):
            both = acc0[block, piece] + recv0[block, piece].astype(F32)
            px, py = 2 * block + piece // 4, piece % 4
            first = py + other * (px - py)
            second = px + other * (py - px)
            part_f32[first, second] = both
            part_low[first, second] = both.astype(FIRST_SUM)
    for k in (2, 1, 3):
        goal = (two + k) % 4
        push(part_low.at[goal], recv1.at[two], R1 + two, chip(one, goal))

    active1 = dot_nt(near1[0], weights[0])
    active1 = active1 + dot_nt(near1[1], weights[1])
    active1 = active1 + dot_nt(near1[2], weights[2])
    own_code, own_flip = code[160:288], flip[160:288]
    slope_f = jnp.zeros((CAP, C), F32)
    slope_r = jnp.zeros((CAP, C), F32)
    for base in range(4):
        slope_f = jnp.where(own_code == base + 1.0, slope0[base : base + 1], slope_f)
        slope_r = jnp.where(own_flip == base + 1.0, slope0[base : base + 1], slope_r)
    start_f = grad1[16:144] + active1[0:128] * slope_f
    start_r = grad1[176:304] + active1[128:256] * slope_r
    exact = lax.Precision.HIGHEST
    contract = (((1,), (1,)), ((), ()))
    score = lax.dot_general(
        emb_fwd[...], start_f, contract, precision=exact, preferred_element_type=F32
    ) + lax.dot_general(
        emb_rev[...], start_r, contract, precision=exact, preferred_element_type=F32
    )
    score = jnp.where(lane < live_count, score, 0.0) * (1.0 / math.sqrt(C))
    sal_ref[0] = score[0:4]

    for k in (1, 2, 3):
        source = (two + k) % 4
        arrive(recv1.at[source], R1 + source)
    total = part_f32[two]
    for k in (1, 2, 3):
        total = total + recv1[(two + k) % 4].astype(F32)
    part2[...] = total
    for k in (2, 1, 3):
        goal = (one + k) % 4
        push(part2.at[goal], recv2.at[one], R2 + one, chip(goal, two))
    for k in (1, 2, 3):
        source = (one + k) % 4
        arrive(recv2.at[source], R2 + source)
    total = part2[one]
    for k in (1, 2, 3):
        total = total + recv2[(one + k) % 4]
    for k in range(16):
        part3[k] = total[k : k + 1]
    place = zl * 2 + zh
    for k in (8, 7, 9, 6, 10, 5, 11, 4, 12, 3, 13, 2, 14, 1, 15):
        goal = (z + k) % 16
        push(part3.at[goal % 8 * 2 + goal // 8], recv3.at[place], R3 + place, along_z(goal))
    for k in range(1, 16):
        source = (place + k) % 16
        arrive(recv3.at[source], R3 + source)
    total = part3[place]
    for k in range(1, 16):
        total = total + recv3[(place + k) % 16]
    grad_ref[...] = total * (1.0 / 256.0)

    for copy in started:
        copy.wait_send()


def shards(bases, lengths, cotangent, conv1, proj1, conv2, proj2, embed):
    vmem = pl.BlockSpec(memory_space=pltpu.VMEM)
    saliency, grad = pl.pallas_call(
        kernel,
        out_shape=(
            jax.ShapeDtypeStruct((1, 4, CAP), F32),
            jax.ShapeDtypeStruct((1, 1152), F32),
        ),
        in_specs=[vmem] * 11,
        out_specs=(vmem, vmem),
        scratch_shapes=[
            pltpu.VMEM((32, B), F32),
            pltpu.VMEM((32, B), BF16),
            pltpu.VMEM((8, 32, B), BF16),
            pltpu.VMEM((8, C, B), BF16),
            pltpu.VMEM((80, C), BF16),
            pltpu.VMEM((128, C), BF16),
            pltpu.VMEM((128, C), BF16),
            pltpu.VMEM((8, CAP), F32),
            pltpu.VMEM((6, 8, CAP), F32),
            pltpu.VMEM((8, C), F32),
            pltpu.VMEM((8, C), F32),
            pltpu.VMEM((2, 8, 16, 1152), CORE_SUM),
            pltpu.VMEM((2, 8, 16, 1152), CORE_SUM),
            pltpu.VMEM((2, 8, 16, 1152), F32),
            pltpu.VMEM((4, 4, 16, 1152), F32),
            pltpu.VMEM((4, 4, 16, 1152), FIRST_SUM),
            pltpu.VMEM((4, 4, 16, 1152), FIRST_SUM),
            pltpu.VMEM((4, 16, 1152), F32),
            pltpu.VMEM((4, 16, 1152), F32),
            pltpu.VMEM((16, 1, 1152), F32),
            pltpu.VMEM((16, 1, 1152), F32),
            pltpu.SemaphoreType.DMA((80,)),
            pltpu.SemaphoreType.DMA((80,)),
        ],
        compiler_params=pltpu.CompilerParams(
            collective_id=0, has_side_effects=True, vmem_limit_bytes=60 * 1024 * 1024
        ),
    )(
        bases,
        lengths,
        cotangent,
        conv1,
        proj1,
        conv2,
        proj2,
        embed,
        jnp.asarray(shard_order(), BF16),
        jnp.asarray(class_order(), BF16),
        jnp.asarray(triple_codes(), F32),
    )
    return saliency, grad.reshape(1152)


def solution(mesh):
    in_specs = (
        P("dp", "seq"),
        P("dp", "seq"),
        P("dp", "seq", None),
        P(None, "seq", None),
        P("seq", None),
        P(None, "seq", None),
        P("seq", None),
        P(),
    )
    out_specs = (P("dp", None, "seq"), P(("seq", "dp")))
    return jax.shard_map(shards, mesh=mesh, in_specs=in_specs, out_specs=out_specs, check_vma=False)
```

```python
import math

import jax
import jax.numpy as jnp
import numpy as np
from jax import lax
from jax.experimental import pallas as pl
from jax.experimental.pallas import tpu as pltpu
from jax.sharding import PartitionSpec as P

MESH = pl.DeviceIdType.MESH
F32 = jnp.float32
BF16 = jnp.bfloat16
C = 768
B = 384
CAP = 128
SQRT_HALF = 0.7071067811865476
INV_SQRT_TWO_PI = 0.3989422804014327
CORE_SUM = BF16
FIRST_SUM = BF16
SECOND_SUM = BF16
FAR = 1.0e6


def shard_order():
    table = np.zeros((192, 192), np.float32)
    for row in range(192):
        piece, within = divmod(row, 48)
        if piece < 3:
            source = within // 6 * 24 + piece * 6 + within % 6
        else:
            half, rest = divmod(within, 24)
            source = rest // 3 * 24 + 18 + half * 3 + rest % 3
        table[row, source] = 1.0
    return table


def class_order():
    table = np.zeros((B, B), np.float32)
    for row in range(B):
        table[row, row % 3 * 128 + row // 3] = 1.0
    return table


def triple_codes():
    table = np.zeros((128, 128), np.float32)
    for row in range(125):
        table[row, :3] = row // 25, row // 5 % 5, row % 5
    return table


def gelu_pair(values):
    bell = 1.0 + lax.erf(values * SQRT_HALF)
    slope = 0.5 * bell + values * jnp.exp(-0.5 * values * values) * INV_SQRT_TWO_PI
    return 0.5 * values * bell, slope


def dot(left, right):
    return jnp.dot(left, right, preferred_element_type=F32)


def dot_nt(left, right):
    return lax.dot_general(left, right, (((1,), (1,)), ((), ())), preferred_element_type=F32)


def dot_tn(left, right):
    return lax.dot_general(left, right, (((0,), (0,)), ((), ())), preferred_element_type=F32)


def halves(values):
    high = values.astype(BF16)
    return high, (values - high.astype(F32)).astype(BF16)


def pick(onehot, pair):
    return dot(onehot, pair[0]) + dot(onehot, pair[1])


def ones_where(mask):
    return jnp.where(mask, 1.0, 0.0)


def iota(shape, dim):
    return lax.broadcasted_iota(jnp.int32, shape, dim)


def kernel(
    bases_hbm,
    len_hbm,
    cot_hbm,
    conv1_hbm,
    proj1_hbm,
    conv2_hbm,
    proj2_hbm,
    embed_hbm,
    order_hbm,
    class_hbm,
    codes_hbm,
    sal_ref,
    grad_ref,
    bases_ref,
    len_ref,
    cot_ref,
    conv1_ref,
    proj1_ref,
    conv2_ref,
    proj2_ref,
    embed_ref,
    order_ref,
    class_ref,
    codes_ref,
    pack32,
    shard,
    zbuf,
    weights,
    tail,
    left_rows,
    right_rows,
    enc_own,
    enc_all,
    emb_fwd,
    emb_rev,
    send0,
    recv0,
    acc0,
    part_f32,
    part_low,
    recv1,
    part2,
    recv2,
    part2_f32,
    part3,
    recv3,
    send_sem,
    recv_sem,
    copy_sem,
    known_sem,
):
    seq = lax.axis_index("seq")
    dpi = lax.axis_index("dp")
    x, y, zl = seq // 32, seq // 8 % 4, seq % 8
    zh, core = dpi // 2, dpi % 2
    z = zh * 8 + zl
    other = 1 - core
    one = y + core * (x - y)
    two = x + core * (y - x)

    def chip(first, second):
        cx = second + core * (first - second)
        cy = first + core * (second - first)
        return ((cx * 4 + cy) * 8 + zl, dpi)

    def along_z(target):
        return ((x * 4 + y) * 8 + target % 8, target // 8 * 2 + core)

    def along_seq(offset):
        return ((seq + offset + 128) % 128, dpi)

    sibling = (seq, zh * 2 + other)

    barrier = pltpu.get_barrier_semaphore()
    line_x = [(((x + k) % 4 * 4 + y) * 8 + zl, dpi) for k in (1, 3)]
    line_y = [((x * 4 + (y + k) % 4) * 8 + zl, dpi) for k in (1, 3)]
    near_z = [along_z((z + k) % 16) for k in (2, 14)]
    far_z = [along_z((z + k) % 16) for k in (4, 12)]
    partners = [sibling] + line_x + line_y + near_z
    partners += [along_z((z + k) % 16) for k in (1, 15)]
    for device in partners:
        pl.semaphore_signal(barrier, inc=1, device_id=device, device_id_type=MESH)

    loads = []
    for k, (source, target) in enumerate(
        (
            (conv1_hbm, conv1_ref),
            (conv2_hbm, conv2_ref),
            (proj1_hbm, proj1_ref),
            (proj2_hbm, proj2_ref),
            (len_hbm, len_ref),
            (bases_hbm, bases_ref),
            (embed_hbm, embed_ref),
            (cot_hbm, cot_ref),
            (order_hbm, order_ref),
            (class_hbm, class_ref),
            (codes_hbm, codes_ref),
        )
    ):
        copy = pltpu.make_async_copy(source, target, copy_sem.at[k])
        copy.start()
        loads.append(copy)

    def announce(devices, slot):
        for device in devices:
            pl.semaphore_signal(
                known_sem.at[slot], inc=1, device_id=device, device_id_type=MESH
            )

    def heard(slot):
        pl.semaphore_wait(known_sem.at[slot], 2)

    used = {"send": 0}
    started = []

    def push(source, target, slot, device):
        copy = pltpu.make_async_remote_copy(
            src_ref=source,
            dst_ref=target,
            send_sem=send_sem.at[used["send"]],
            recv_sem=recv_sem.at[slot],
            device_id=device,
            device_id_type=MESH,
        )
        used["send"] += 1
        copy.start()
        started.append(copy)

    def arrive(target, slot):
        pltpu.make_async_remote_copy(
            src_ref=target,
            dst_ref=target,
            send_sem=send_sem.at[0],
            recv_sem=recv_sem.at[slot],
            device_id=sibling,
            device_id_type=MESH,
        ).wait_recv()

    for copy in loads:
        copy.wait()
    lane = iota((1, CAP), 1)
    live_count = len_ref[0, 0]
    code_row = jnp.where(lane < live_count, bases_ref[...] + 1, 0).astype(F32)
    enc_own[...] = jnp.broadcast_to(code_row, (8, CAP))
    own_cot = cot_ref[0]
    choose = iota((80, CAP), 1) - iota((80, CAP), 0) == live_count - 80
    tail[...] = dot(ones_where(choose).astype(BF16), own_cot).astype(BF16)
    left_rows[96:128] = jnp.zeros((32, C), BF16)
    right_rows[96:128] = jnp.zeros((32, C), BF16)
    first_core = core == 0
    for k in range(3):
        pack32[6 * k : 6 * k + 6] = jnp.where(
            first_core, conv1_ref[k].astype(F32), conv2_ref[k].astype(F32)
        )
    proj_rows = jnp.where(first_core, proj1_ref[...].astype(F32), proj2_ref[...].astype(F32))
    pack32[18:21] = proj_rows[:, :B]
    pack32[21:24] = proj_rows[:, B:]
    shard[...] = pack32[...].astype(BF16)
    zbuf[zl] = pack32[...].astype(BF16)
    emb_fwd[0:4] = embed_ref[...]
    emb_fwd[4:8] = jnp.zeros((4, C), F32)
    emb_rev[4:8] = jnp.zeros((4, C), F32)
    for k in range(4):
        emb_rev[k : k + 1] = embed_ref[3 - k : 4 - k]

    pl.semaphore_wait(barrier, len(partners))

    Z, D1F, D1H, D2F, D2H, SIB, HALO, ENC, R0, R1, R2, R3 = (
        0, 8, 10, 12, 20, 28, 44, 48, 54, 56, 60, 64,
    )
    turn_z = 1 - 2 * core

    def z_at(offset):
        return along_z((z + offset * turn_z + 16) % 16)

    def z_slot(offset):
        return (zl + offset * turn_z + 8) % 8

    def z_wait(offset):
        arrive(zbuf.at[z_slot(offset)], Z + z_slot(offset))

    def z_pass(offset, onward):
        z_wait(offset)
        held = zbuf.at[z_slot(offset)]
        push(held, held, Z + z_slot(offset), z_at(onward))

    for offset in (2, -2, 1, -1):
        push(shard, zbuf.at[zl], Z + zl, z_at(offset))
    announce(near_z, 0)
    z_pass(-1, 2)
    z_pass(1, -2)
    z_pass(-2, 2)
    heard(0)
    announce(far_z, 1)
    for offset in (2, 3, -3, -4):
        z_wait(offset)

    def block_of(owner, first, second, piece, count):
        group = first * (1 + 3 * owner) + second * (4 - 3 * owner)
        rows = pl.ds(pl.multiple_of(group * 48, 16), 48)
        return weights.at[pl.ds(4 * owner + piece, count), rows, :]

    gathered = zbuf[...].astype(F32).reshape(192, B).astype(BF16)
    moved = dot(order_ref[...], gathered).astype(BF16)
    own_rows = pl.ds(pl.multiple_of((x * 4 + y) * 48, 16), 48)
    for k in range(4):
        weights[4 * core + k, own_rows, :] = moved[48 * k : 48 * k + 48]

    steps = (0, 3, 1, 2)

    def line(step, turn, piece=0, count=4):
        return block_of(core, (one + steps[step]) % 4, (two + steps[turn]) % 4, piece, count)

    one_up, one_down = chip((one + 1) % 4, two), chip((one + 3) % 4, two)
    two_up, two_down = chip(one, (two + 1) % 4), chip(one, (two + 3) % 4)

    def to_sibling(step, turn):
        push(line(step, turn), line(step, turn), SIB + step * 4 + turn, sibling)

    def to_second(step):
        push(line(step, 0), line(step, 0), D2F + step * 2, two_up)
        push(line(step, 0), line(step, 0), D2F + step * 2 + 1, two_down)

    def relay_second(step):
        arrive(line(step, 1), D2F + step * 2)
        push(line(step, 1, 0, 2), line(step, 1, 0, 2), D2H + step * 2, two_up)
        to_sibling(step, 1)
        arrive(line(step, 2), D2F + step * 2 + 1)
        push(line(step, 2, 2, 2), line(step, 2, 2, 2), D2H + step * 2 + 1, two_down)
        to_sibling(step, 2)

    push(line(0, 0), line(0, 0), D1F, one_up)
    push(line(0, 0), line(0, 0), D1F + 1, one_down)
    to_second(0)
    to_sibling(0, 0)
    heard(1)
    announce(line_x, 2)
    arrive(line(1, 0), D1F)
    push(line(1, 0, 0, 2), line(1, 0, 0, 2), D1H, one_up)
    to_second(1)
    to_sibling(1, 0)
    arrive(line(2, 0), D1F + 1)
    push(line(2, 0, 2, 2), line(2, 0, 2, 2), D1H + 1, one_down)
    to_second(2)
    to_sibling(2, 0)
    heard(2)
    announce(line_y, 3)
    relay_second(0)
    heard(3)
    for k in (1, 2, 3):
        push(enc_own, enc_all.at[k - 1], ENC + k - 1, along_seq(k))
        push(enc_own, enc_all.at[2 + k], ENC + 2 + k, along_seq(-k))
    push(tail, left_rows.at[0:80], HALO, along_seq(1))
    push(cot_ref.at[0, 0:80], right_rows.at[0:80], HALO + 1, along_seq(-1))
    push(tail.at[64:80], left_rows.at[80:96], HALO + 2, along_seq(2))
    push(cot_ref.at[0, 0:16], right_rows.at[80:96], HALO + 3, along_seq(-2))
    arrive(line(3, 0, 0, 2), D1H)
    arrive(line(3, 0, 2, 2), D1H + 1)
    to_second(3)
    to_sibling(3, 0)
    for step in (1, 2, 3):
        relay_second(step)
    for step in range(4):
        arrive(line(step, 3, 0, 2), D2H + step * 2)
        arrive(line(step, 3, 2, 2), D2H + step * 2 + 1)
        to_sibling(step, 3)

    for k in range(6):
        arrive(enc_all.at[k], ENC + k)
    own_n = jnp.sum(ones_where(code_row > 0.0), axis=1, keepdims=True)
    lane_f = lane.astype(F32)
    rows_t = (iota((448, 1), 0) - 160).astype(F32)
    pieces = [(code_row, jnp.zeros((1, 1), F32))]
    left_n, right_n = [], []
    left_at, right_at = jnp.zeros((1, 1), F32), own_n
    for k in (1, 2, 3):
        there = jnp.where(seq >= k, 1.0, 0.0)
        row = enc_all[k - 1, 0:1] * there
        count = jnp.sum(ones_where(row > 0.0), axis=1, keepdims=True)
        left_at = left_at - count
        left_n.append(count)
        pieces.append((row, left_at))
        there = jnp.where(seq + k <= 127, 1.0, 0.0)
        row = enc_all[2 + k, 0:1] * there
        count = jnp.sum(ones_where(row > 0.0), axis=1, keepdims=True)
        pieces.append((row, right_at))
        right_at = right_at + count
        right_n.append(count)
    found = jnp.zeros((448, CAP), F32)
    for row, start in pieces:
        found = found + jnp.where(rows_t == lane_f + start, row, 0.0)
    code = jnp.sum(found, axis=1, keepdims=True)
    flip = jnp.where(code > 0.0, 5.0 - code, 0.0)
    triple_f = 25.0 * code[0:416] + 5.0 * code[16:432] + code[32:448]
    triple_r = 25.0 * flip[32:448] + 5.0 * flip[16:432] + flip[0:416]
    hot_f = ones_where(triple_f == lane_f).astype(BF16)
    hot_r = ones_where(triple_r == lane_f).astype(BF16)

    for step in range(4):
        for turn in range(4):
            theirs = block_of(
                other,
                (x + core * (y - x) + steps[step]) % 4,
                (y + core * (x - y) + steps[turn]) % 4,
                0,
                4,
            )
            arrive(theirs, SIB + step * 4 + turn)

    def projection(block):
        rows = weights[4 * block + 3].astype(F32).reshape(16, 2, 24, B)
        return [rows[:, half].reshape(B, B).astype(BF16) for half in range(2)]

    proj1 = jnp.concatenate(projection(0), axis=1)
    proj2 = jnp.concatenate(projection(1), axis=1)

    before_code, mid_code, after_code = codes_ref[:, 0:1], codes_ref[:, 1:2], codes_ref[:, 2:3]
    value0, slope0 = gelu_pair(emb_fwd[...])
    low0 = value0.astype(BF16)
    hidden1 = jnp.zeros((128, B), F32)
    for k, column in enumerate((before_code, mid_code, after_code)):
        rows = dot(low0, weights[k])
        for base in range(4):
            hidden1 = hidden1 + jnp.where(column == base + 1.0, rows[base : base + 1], 0.0)
    table_live = ones_where(mid_code > 0.0)
    hidden1 = hidden1 * table_live
    value1, slope1 = gelu_pair(hidden1)
    mid1 = value1.astype(BF16)
    slope1 = halves(slope1 * table_live)
    stream1 = jnp.zeros((128, C), F32)
    for base in range(4):
        stream1 = stream1 + jnp.where(mid_code == base + 1.0, emb_fwd[base : base + 1], 0.0)
    stream1 = stream1 + dot(mid1, proj1)
    value_x, slope_x = gelu_pair(stream1)
    low_x = (value_x * table_live).astype(BF16)
    slope_x = halves(slope_x * table_live)
    taps2 = halves(jnp.concatenate([dot(low_x, weights[4 + k]) for k in range(3)], axis=0))

    arrive(left_rows.at[0:80], HALO)
    arrive(right_rows.at[0:80], HALO + 1)
    arrive(left_rows.at[80:96], HALO + 2)
    arrive(right_rows.at[80:96], HALO + 3)
    t288 = (iota((288, 1), 0) - 80).astype(F32)
    own_pos = jnp.where(lane_f < own_n, lane_f, FAR)
    left_pos = jnp.where(lane_f >= 80.0 - left_n[0], lane_f - 80.0, FAR)
    left_far = jnp.where(left_n[1] > 0.0, lane_f - 96.0 - left_n[0], FAR)
    left_pos = jnp.where(lane_f < 80.0, left_pos, jnp.where(lane_f < 96.0, left_far, FAR))
    right_pos = jnp.where(lane_f < right_n[0], lane_f + own_n, FAR)
    right_far = jnp.where(right_n[1] > 0.0, lane_f - 80.0 + own_n + right_n[0], FAR)
    right_pos = jnp.where(lane_f < 80.0, right_pos, jnp.where(lane_f < 96.0, right_far, FAR))
    cot = (
        dot(ones_where(t288 == own_pos).astype(BF16), own_cot)
        + dot(ones_where(t288 == left_pos).astype(BF16), left_rows[...])
        + dot(ones_where(t288 == right_pos).astype(BF16), right_rows[...])
    )
    grad2 = 0.5 * cot
    grad2_low = grad2.astype(BF16)

    hot2 = jnp.concatenate(
        [
            jnp.concatenate([hot_f[0:288], hot_f[64:352], hot_f[128:416]], axis=1),
            jnp.concatenate([hot_r[128:416], hot_r[64:352], hot_r[0:288]], axis=1),
        ],
        axis=0,
    )
    hidden2 = pick(hot2, taps2)
    value2, slope2 = gelu_pair(hidden2)
    live288 = ones_where(code[80:368] > 0.0)
    back2 = dot_nt(grad2_low, proj2) * live288
    own_mask = ones_where(iota((CAP, 1), 0).astype(F32) < own_n)
    mid2 = jnp.concatenate([value2[80:208] * own_mask, value2[368:496] * own_mask], axis=0)
    classes = class_ref[...]
    mid2 = dot(mid2.astype(BF16), classes).astype(BF16)
    own_grad2 = grad2_low[80:208]
    sum2 = dot_tn(mid2, jnp.concatenate([own_grad2, own_grad2], axis=0))

    def to_core(block, total):
        first = jnp.concatenate([total[0:128], total[128:256, 0:B]], axis=1)
        second = jnp.concatenate([total[128:256, B:], total[256:384]], axis=1)
        send0[block] = jnp.where(first_core, second, first).astype(CORE_SUM).reshape(8, 16, 1152)
        acc0[block] = jnp.where(first_core, first, second).reshape(8, 16, 1152)
        push(send0.at[block], recv0.at[block], R0 + block, sibling)

    to_core(1, sum2)
    gh_f = (back2 * slope2[0:288]).astype(BF16)
    gh_r = (back2 * slope2[288:576]).astype(BF16)
    near2 = [
        jnp.concatenate([gh_f[128:288], gh_r[0:160]], axis=0),
        jnp.concatenate([gh_f[64:224], gh_r[64:224]], axis=0),
        jnp.concatenate([gh_f[0:160], gh_r[128:288]], axis=0),
    ]
    active2 = dot_nt(near2[0], weights[4])
    active2 = active2 + dot_nt(near2[1], weights[5])
    active2 = active2 + dot_nt(near2[2], weights[6])
    hot1 = jnp.concatenate([hot_f[128:288], hot_r[128:288]], axis=0)
    around = grad2[64:224]
    grad1 = jnp.concatenate([around, around], axis=0) + active2 * pick(hot1, slope_x)
    grad1_low = grad1.astype(BF16)

    own_low = own_mask.astype(BF16)
    own_hot = jnp.concatenate([hot_f[144:272] * own_low, hot_r[144:272] * own_low], axis=0)
    mid1 = dot(own_hot, dot(mid1, classes).astype(BF16)).astype(BF16)
    sum1 = dot_tn(mid1, jnp.concatenate([grad1_low[16:144], grad1_low[176:304]], axis=0))
    to_core(0, sum1)
    back1 = dot_nt(grad1_low, proj1)
    gh1 = (back1 * pick(hot1, slope1)).astype(BF16)
    near1 = [
        jnp.concatenate([gh1[32:160], gh1[160:288]], axis=0),
        jnp.concatenate([gh1[16:144], gh1[176:304]], axis=0),
        jnp.concatenate([gh1[0:128], gh1[192:320]], axis=0),
    ]

    for block in (1, 0):
        arrive(recv0.at[block], R0 + block)
        for piece in range(8):
            both = acc0[block, piece] + recv0[block, piece].astype(F32)
            px, py = 2 * block + piece // 4, piece % 4
            first = py + other * (px - py)
            second = px + other * (py - px)
            part_f32[first, second] = both
            part_low[first, second] = both.astype(FIRST_SUM)
    for k in (2, 1, 3):
        goal = (two + k) % 4
        push(part_low.at[goal], recv1.at[two], R1 + two, chip(one, goal))

    active1 = dot_nt(near1[0], weights[0])
    active1 = active1 + dot_nt(near1[1], weights[1])
    active1 = active1 + dot_nt(near1[2], weights[2])
    own_code, own_flip = code[160:288], flip[160:288]
    slope_f = jnp.zeros((CAP, C), F32)
    slope_r = jnp.zeros((CAP, C), F32)
    for base in range(4):
        slope_f = jnp.where(own_code == base + 1.0, slope0[base : base + 1], slope_f)
        slope_r = jnp.where(own_flip == base + 1.0, slope0[base : base + 1], slope_r)
    start_f = grad1[16:144] + active1[0:128] * slope_f
    start_r = grad1[176:304] + active1[128:256] * slope_r
    exact = lax.Precision.HIGHEST
    contract = (((1,), (1,)), ((), ()))
    score = lax.dot_general(
        emb_fwd[...], start_f, contract, precision=exact, preferred_element_type=F32
    ) + lax.dot_general(
        emb_rev[...], start_r, contract, precision=exact, preferred_element_type=F32
    )
    score = jnp.where(lane < live_count, score, 0.0) * (1.0 / math.sqrt(C))
    sal_ref[0] = score[0:4]

    for k in (1, 2, 3):
        source = (two + k) % 4
        arrive(recv1.at[source], R1 + source)
    total = part_f32[two]
    for k in (1, 2, 3):
        total = total + recv1[(two + k) % 4].astype(F32)
    part2_f32[...] = total
    part2[...] = total.astype(SECOND_SUM)
    for k in (2, 1, 3):
        goal = (one + k) % 4
        push(part2.at[goal], recv2.at[one], R2 + one, chip(goal, two))
    for k in (1, 2, 3):
        source = (one + k) % 4
        arrive(recv2.at[source], R2 + source)
    total = part2_f32[one]
    for k in (1, 2, 3):
        total = total + recv2[(one + k) % 4].astype(F32)
    for k in range(16):
        part3[k] = total[k : k + 1]
    place = zl * 2 + zh
    for k in (8, 7, 9, 6, 10, 5, 11, 4, 12, 3, 13, 2, 14, 1, 15):
        goal = (z + k) % 16
        push(part3.at[goal % 8 * 2 + goal // 8], recv3.at[place], R3 + place, along_z(goal))
    for k in range(1, 16):
        source = (place + k) % 16
        arrive(recv3.at[source], R3 + source)
    total = part3[place]
    for k in range(1, 16):
        total = total + recv3[(place + k) % 16]
    grad_ref[...] = total * (1.0 / 256.0)

    for copy in started:
        copy.wait_send()


def shards(bases, lengths, cotangent, conv1, proj1, conv2, proj2, embed):
    vmem = pl.BlockSpec(memory_space=pltpu.VMEM)
    saliency, grad = pl.pallas_call(
        kernel,
        out_shape=(
            jax.ShapeDtypeStruct((1, 4, CAP), F32),
            jax.ShapeDtypeStruct((1, 1152), F32),
        ),
        in_specs=[pl.BlockSpec(memory_space=pl.ANY)] * 11,
        out_specs=(vmem, vmem),
        scratch_shapes=[
            pltpu.VMEM((1, CAP), jnp.int32),
            pltpu.SMEM((1, 1), jnp.int32),
            pltpu.VMEM((1, CAP, C), BF16),
            pltpu.VMEM((3, 6, B), BF16),
            pltpu.VMEM((3, C), BF16),
            pltpu.VMEM((3, 6, B), BF16),
            pltpu.VMEM((3, C), BF16),
            pltpu.VMEM((4, C), F32),
            pltpu.VMEM((192, 192), BF16),
            pltpu.VMEM((B, B), BF16),
            pltpu.VMEM((128, 128), F32),
            pltpu.VMEM((24, B), F32),
            pltpu.VMEM((24, B), BF16),
            pltpu.VMEM((8, 24, B), BF16),
            pltpu.VMEM((8, C, B), BF16),
            pltpu.VMEM((80, C), BF16),
            pltpu.VMEM((128, C), BF16),
            pltpu.VMEM((128, C), BF16),
            pltpu.VMEM((8, CAP), F32),
            pltpu.VMEM((6, 8, CAP), F32),
            pltpu.VMEM((8, C), F32),
            pltpu.VMEM((8, C), F32),
            pltpu.VMEM((2, 8, 16, 1152), CORE_SUM),
            pltpu.VMEM((2, 8, 16, 1152), CORE_SUM),
            pltpu.VMEM((2, 8, 16, 1152), F32),
            pltpu.VMEM((4, 4, 16, 1152), F32),
            pltpu.VMEM((4, 4, 16, 1152), FIRST_SUM),
            pltpu.VMEM((4, 4, 16, 1152), FIRST_SUM),
            pltpu.VMEM((4, 16, 1152), SECOND_SUM),
            pltpu.VMEM((4, 16, 1152), SECOND_SUM),
            pltpu.VMEM((4, 16, 1152), F32),
            pltpu.VMEM((16, 1, 1152), F32),
            pltpu.VMEM((16, 1, 1152), F32),
            pltpu.SemaphoreType.DMA((80,)),
            pltpu.SemaphoreType.DMA((80,)),
            pltpu.SemaphoreType.DMA((11,)),
            pltpu.SemaphoreType.REGULAR((4,)),
        ],
        compiler_params=pltpu.CompilerParams(
            collective_id=0, has_side_effects=True, vmem_limit_bytes=60 * 1024 * 1024
        ),
    )(
        bases,
        lengths,
        cotangent,
        conv1,
        proj1,
        conv2,
        proj2,
        embed,
        jnp.asarray(shard_order(), BF16),
        jnp.asarray(class_order(), BF16),
        jnp.asarray(triple_codes(), F32),
    )
    return saliency, grad.reshape(1152)


def solution(mesh):
    in_specs = (
        P("dp", "seq"),
        P("dp", "seq"),
        P("dp", "seq", None),
        P(None, "seq", None),
        P("seq", None),
        P(None, "seq", None),
        P("seq", None),
        P(),
    )
    out_specs = (P("dp", None, "seq"), P(("seq", "dp")))
    return jax.shard_map(shards, mesh=mesh, in_specs=in_specs, out_specs=out_specs, check_vma=False)
```

```python
import math

import jax
import jax.numpy as jnp
import numpy as np
from jax import lax
from jax.experimental import pallas as pl
from jax.experimental.pallas import tpu as pltpu
from jax.sharding import PartitionSpec as P

MESH = pl.DeviceIdType.MESH
F32 = jnp.float32
BF16 = jnp.bfloat16
C = 768
B = 384
CAP = 128
SQRT_HALF = 0.7071067811865476
INV_SQRT_TWO_PI = 0.3989422804014327
CORE_SUM = BF16
FIRST_SUM = BF16
SECOND_SUM = BF16
FAR = 1.0e6


def shard_order():
    table = np.zeros((192, 192), np.float32)
    for row in range(192):
        piece, within = divmod(row, 48)
        if piece < 3:
            source = within // 6 * 24 + piece * 6 + within % 6
        else:
            half, rest = divmod(within, 24)
            source = rest // 3 * 24 + 18 + half * 3 + rest % 3
        table[row, source] = 1.0
    return table


def class_order():
    table = np.zeros((B, B), np.float32)
    for row in range(B):
        table[row, row % 3 * 128 + row // 3] = 1.0
    return table


def triple_codes():
    table = np.zeros((128, 128), np.float32)
    for row in range(125):
        table[row, :3] = row // 25, row // 5 % 5, row % 5
    return table


def gelu_pair(values):
    bell = 1.0 + lax.erf(values * SQRT_HALF)
    slope = 0.5 * bell + values * jnp.exp(-0.5 * values * values) * INV_SQRT_TWO_PI
    return 0.5 * values * bell, slope


def dot(left, right):
    return jnp.dot(left, right, preferred_element_type=F32)


def dot_nt(left, right):
    return lax.dot_general(left, right, (((1,), (1,)), ((), ())), preferred_element_type=F32)


def dot_tn(left, right):
    return lax.dot_general(left, right, (((0,), (0,)), ((), ())), preferred_element_type=F32)


def halves(values):
    high = values.astype(BF16)
    return high, (values - high.astype(F32)).astype(BF16)


def pick(onehot, pair):
    return dot(onehot, pair[0]) + dot(onehot, pair[1])


def ones_where(mask):
    return jnp.where(mask, 1.0, 0.0)


def iota(shape, dim):
    return lax.broadcasted_iota(jnp.int32, shape, dim)


def kernel(
    bases_hbm,
    len_hbm,
    cot_hbm,
    conv1_hbm,
    proj1_hbm,
    conv2_hbm,
    proj2_hbm,
    embed_hbm,
    order_hbm,
    class_hbm,
    codes_hbm,
    sal_ref,
    grad_ref,
    bases_ref,
    len_ref,
    cot_ref,
    conv1_ref,
    proj1_ref,
    conv2_ref,
    proj2_ref,
    embed_ref,
    order_ref,
    class_ref,
    codes_ref,
    pack32,
    shard,
    zbuf,
    weights,
    tail,
    left_rows,
    right_rows,
    enc_own,
    enc_all,
    emb_fwd,
    emb_rev,
    send0,
    recv0,
    acc0,
    part_f32,
    part_low,
    recv1,
    part2,
    recv2,
    part2_f32,
    part3,
    recv3,
    send_sem,
    recv_sem,
    copy_sem,
    known_sem,
):
    seq = lax.axis_index("seq")
    dpi = lax.axis_index("dp")
    x, y, zl = seq // 32, seq // 8 % 4, seq % 8
    zh, core = dpi // 2, dpi % 2
    z = zh * 8 + zl
    other = 1 - core
    one = y + core * (x - y)
    two = x + core * (y - x)

    def chip(first, second):
        cx = second + core * (first - second)
        cy = first + core * (second - first)
        return ((cx * 4 + cy) * 8 + zl, dpi)

    def along_z(target):
        return ((x * 4 + y) * 8 + target % 8, target // 8 * 2 + core)

    def along_seq(offset):
        return ((seq + offset + 128) % 128, dpi)

    sibling = (seq, zh * 2 + other)

    barrier = pltpu.get_barrier_semaphore()
    line_x = [(((x + k) % 4 * 4 + y) * 8 + zl, dpi) for k in (1, 3)]
    line_y = [((x * 4 + (y + k) % 4) * 8 + zl, dpi) for k in (1, 3)]
    near_z = [along_z((z + k) % 16) for k in (2, 14)]
    far_z = [along_z((z + k) % 16) for k in (4, 12)]
    partners = [sibling] + line_x + line_y + near_z
    partners += [along_z((z + k) % 16) for k in (1, 15)]
    for device in partners:
        pl.semaphore_signal(barrier, inc=1, device_id=device, device_id_type=MESH)

    loads = []
    for k, (source, target) in enumerate(
        (
            (conv1_hbm, conv1_ref),
            (conv2_hbm, conv2_ref),
            (proj1_hbm, proj1_ref),
            (proj2_hbm, proj2_ref),
            (len_hbm, len_ref),
            (bases_hbm, bases_ref),
            (embed_hbm, embed_ref),
            (cot_hbm, cot_ref),
            (order_hbm, order_ref),
            (class_hbm, class_ref),
            (codes_hbm, codes_ref),
        )
    ):
        copy = pltpu.make_async_copy(source, target, copy_sem.at[k])
        copy.start()
        loads.append(copy)

    def announce(devices, slot):
        for device in devices:
            pl.semaphore_signal(
                known_sem.at[slot], inc=1, device_id=device, device_id_type=MESH
            )

    def heard(slot):
        pl.semaphore_wait(known_sem.at[slot], 2)

    used = {"send": 0}
    started = []

    def push(source, target, slot, device):
        copy = pltpu.make_async_remote_copy(
            src_ref=source,
            dst_ref=target,
            send_sem=send_sem.at[used["send"]],
            recv_sem=recv_sem.at[slot],
            device_id=device,
            device_id_type=MESH,
        )
        used["send"] += 1
        copy.start()
        started.append(copy)

    def arrive(target, slot):
        pltpu.make_async_remote_copy(
            src_ref=target,
            dst_ref=target,
            send_sem=send_sem.at[0],
            recv_sem=recv_sem.at[slot],
            device_id=sibling,
            device_id_type=MESH,
        ).wait_recv()

    for copy in loads:
        copy.wait()
    lane = iota((1, CAP), 1)
    live_count = len_ref[0, 0]
    code_row = jnp.where(lane < live_count, bases_ref[...] + 1, 0).astype(F32)
    enc_own[...] = jnp.broadcast_to(code_row, (8, CAP))
    own_cot = cot_ref[0]
    choose = iota((80, CAP), 1) - iota((80, CAP), 0) == live_count - 80
    tail[...] = dot(ones_where(choose).astype(BF16), own_cot).astype(BF16)
    left_rows[96:128] = jnp.zeros((32, C), BF16)
    right_rows[96:128] = jnp.zeros((32, C), BF16)
    first_core = core == 0
    for k in range(3):
        pack32[6 * k : 6 * k + 6] = jnp.where(
            first_core, conv1_ref[k].astype(F32), conv2_ref[k].astype(F32)
        )
    proj_rows = jnp.where(first_core, proj1_ref[...].astype(F32), proj2_ref[...].astype(F32))
    pack32[18:21] = proj_rows[:, :B]
    pack32[21:24] = proj_rows[:, B:]
    shard[...] = pack32[...].astype(BF16)
    zbuf[zl] = pack32[...].astype(BF16)
    emb_fwd[0:4] = embed_ref[...]
    emb_fwd[4:8] = jnp.zeros((4, C), F32)
    emb_rev[4:8] = jnp.zeros((4, C), F32)
    for k in range(4):
        emb_rev[k : k + 1] = embed_ref[3 - k : 4 - k]

    pl.semaphore_wait(barrier, len(partners))

    Z, D1F, D1H, D2F, D2H, SIB, HALO, ENC, R0, R1, R2, R3 = (
        0, 8, 10, 12, 20, 28, 44, 48, 54, 56, 60, 64,
    )
    turn_z = 1 - 2 * core

    def z_at(offset):
        return along_z((z + offset * turn_z + 16) % 16)

    def z_slot(offset):
        return (zl + offset * turn_z + 8) % 8

    def z_wait(offset):
        arrive(zbuf.at[z_slot(offset)], Z + z_slot(offset))

    def z_pass(offset, onward):
        z_wait(offset)
        held = zbuf.at[z_slot(offset)]
        push(held, held, Z + z_slot(offset), z_at(onward))

    for offset in (2, -2, 1, -1):
        push(shard, zbuf.at[zl], Z + zl, z_at(offset))
    announce(near_z, 0)
    z_pass(-1, 2)
    z_pass(1, -2)
    z_pass(-2, 2)
    heard(0)
    announce(far_z, 1)
    for offset in (2, 3, -3, -4):
        z_wait(offset)

    def block_of(owner, first, second, piece, count):
        group = first * (1 + 3 * owner) + second * (4 - 3 * owner)
        rows = pl.ds(pl.multiple_of(group * 48, 16), 48)
        return weights.at[pl.ds(4 * owner + piece, count), rows, :]

    gathered = zbuf[...].astype(F32).reshape(192, B).astype(BF16)
    moved = dot(order_ref[...], gathered).astype(BF16)
    own_rows = pl.ds(pl.multiple_of((x * 4 + y) * 48, 16), 48)
    for k in range(4):
        weights[4 * core + k, own_rows, :] = moved[48 * k : 48 * k + 48]

    steps = (0, 3, 1, 2)

    def line(step, turn, piece=0, count=4):
        return block_of(core, (one + steps[step]) % 4, (two + steps[turn]) % 4, piece, count)

    one_up, one_down = chip((one + 1) % 4, two), chip((one + 3) % 4, two)
    two_up, two_down = chip(one, (two + 1) % 4), chip(one, (two + 3) % 4)

    def to_sibling(step, turn):
        push(line(step, turn), line(step, turn), SIB + step * 4 + turn, sibling)

    def to_second(step):
        push(line(step, 0), line(step, 0), D2F + step * 2, two_up)
        push(line(step, 0), line(step, 0), D2F + step * 2 + 1, two_down)

    def relay_second(step):
        arrive(line(step, 1), D2F + step * 2)
        push(line(step, 1, 0, 2), line(step, 1, 0, 2), D2H + step * 2, two_up)
        to_sibling(step, 1)
        arrive(line(step, 2), D2F + step * 2 + 1)
        push(line(step, 2, 2, 2), line(step, 2, 2, 2), D2H + step * 2 + 1, two_down)
        to_sibling(step, 2)

    push(line(0, 0), line(0, 0), D1F, one_up)
    push(line(0, 0), line(0, 0), D1F + 1, one_down)
    to_second(0)
    to_sibling(0, 0)
    heard(1)
    announce(line_x, 2)
    arrive(line(1, 0), D1F)
    push(line(1, 0, 0, 2), line(1, 0, 0, 2), D1H, one_up)
    to_second(1)
    to_sibling(1, 0)
    heard(2)
    announce(line_y, 3)
    arrive(line(2, 0), D1F + 1)
    push(line(2, 0, 2, 2), line(2, 0, 2, 2), D1H + 1, one_down)
    to_second(2)
    to_sibling(2, 0)
    heard(3)
    for k in (1, 2, 3):
        push(enc_own, enc_all.at[k - 1], ENC + k - 1, along_seq(k))
        push(enc_own, enc_all.at[2 + k], ENC + 2 + k, along_seq(-k))
    push(tail, left_rows.at[0:80], HALO, along_seq(1))
    push(cot_ref.at[0, 0:80], right_rows.at[0:80], HALO + 1, along_seq(-1))
    push(tail.at[64:80], left_rows.at[80:96], HALO + 2, along_seq(2))
    push(cot_ref.at[0, 0:16], right_rows.at[80:96], HALO + 3, along_seq(-2))
    relay_second(0)
    arrive(line(3, 0, 0, 2), D1H)
    arrive(line(3, 0, 2, 2), D1H + 1)
    to_second(3)
    to_sibling(3, 0)
    for step in (1, 2, 3):
        relay_second(step)
    for step in range(4):
        arrive(line(step, 3, 0, 2), D2H + step * 2)
        arrive(line(step, 3, 2, 2), D2H + step * 2 + 1)
        to_sibling(step, 3)

    for k in range(6):
        arrive(enc_all.at[k], ENC + k)
    own_n = jnp.sum(ones_where(code_row > 0.0), axis=1, keepdims=True)
    lane_f = lane.astype(F32)
    rows_t = (iota((448, 1), 0) - 160).astype(F32)
    pieces = [(code_row, jnp.zeros((1, 1), F32))]
    left_n, right_n = [], []
    left_at, right_at = jnp.zeros((1, 1), F32), own_n
    for k in (1, 2, 3):
        there = jnp.where(seq >= k, 1.0, 0.0)
        row = enc_all[k - 1, 0:1] * there
        count = jnp.sum(ones_where(row > 0.0), axis=1, keepdims=True)
        left_at = left_at - count
        left_n.append(count)
        pieces.append((row, left_at))
        there = jnp.where(seq + k <= 127, 1.0, 0.0)
        row = enc_all[2 + k, 0:1] * there
        count = jnp.sum(ones_where(row > 0.0), axis=1, keepdims=True)
        pieces.append((row, right_at))
        right_at = right_at + count
        right_n.append(count)
    found = jnp.zeros((448, CAP), F32)
    for row, start in pieces:
        found = found + jnp.where(rows_t == lane_f + start, row, 0.0)
    code = jnp.sum(found, axis=1, keepdims=True)
    flip = jnp.where(code > 0.0, 5.0 - code, 0.0)
    triple_f = 25.0 * code[0:416] + 5.0 * code[16:432] + code[32:448]
    triple_r = 25.0 * flip[32:448] + 5.0 * flip[16:432] + flip[0:416]
    hot_f = ones_where(triple_f == lane_f).astype(BF16)
    hot_r = ones_where(triple_r == lane_f).astype(BF16)

    arrive(left_rows.at[0:80], HALO)
    arrive(right_rows.at[0:80], HALO + 1)
    arrive(left_rows.at[80:96], HALO + 2)
    arrive(right_rows.at[80:96], HALO + 3)
    t288 = (iota((288, 1), 0) - 80).astype(F32)
    own_pos = jnp.where(lane_f < own_n, lane_f, FAR)
    left_pos = jnp.where(lane_f >= 80.0 - left_n[0], lane_f - 80.0, FAR)
    left_far = jnp.where(left_n[1] > 0.0, lane_f - 96.0 - left_n[0], FAR)
    left_pos = jnp.where(lane_f < 80.0, left_pos, jnp.where(lane_f < 96.0, left_far, FAR))
    right_pos = jnp.where(lane_f < right_n[0], lane_f + own_n, FAR)
    right_far = jnp.where(right_n[1] > 0.0, lane_f - 80.0 + own_n + right_n[0], FAR)
    right_pos = jnp.where(lane_f < 80.0, right_pos, jnp.where(lane_f < 96.0, right_far, FAR))
    cot = (
        dot(ones_where(t288 == own_pos).astype(BF16), own_cot)
        + dot(ones_where(t288 == left_pos).astype(BF16), left_rows[...])
        + dot(ones_where(t288 == right_pos).astype(BF16), right_rows[...])
    )
    grad2 = 0.5 * cot
    grad2_low = grad2.astype(BF16)

    for step in range(4):
        for turn in range(4):
            theirs = block_of(
                other,
                (x + core * (y - x) + steps[step]) % 4,
                (y + core * (x - y) + steps[turn]) % 4,
                0,
                4,
            )
            arrive(theirs, SIB + step * 4 + turn)

    def projection(block):
        rows = weights[4 * block + 3].astype(F32).reshape(16, 2, 24, B)
        return [rows[:, half].reshape(B, B).astype(BF16) for half in range(2)]

    proj1 = jnp.concatenate(projection(0), axis=1)
    proj2 = jnp.concatenate(projection(1), axis=1)

    before_code, mid_code, after_code = codes_ref[:, 0:1], codes_ref[:, 1:2], codes_ref[:, 2:3]
    value0, slope0 = gelu_pair(emb_fwd[...])
    low0 = value0.astype(BF16)
    hidden1 = jnp.zeros((128, B), F32)
    for k, column in enumerate((before_code, mid_code, after_code)):
        rows = dot(low0, weights[k])
        for base in range(4):
            hidden1 = hidden1 + jnp.where(column == base + 1.0, rows[base : base + 1], 0.0)
    table_live = ones_where(mid_code > 0.0)
    hidden1 = hidden1 * table_live
    value1, slope1 = gelu_pair(hidden1)
    mid1 = value1.astype(BF16)
    slope1 = halves(slope1 * table_live)
    stream1 = jnp.zeros((128, C), F32)
    for base in range(4):
        stream1 = stream1 + jnp.where(mid_code == base + 1.0, emb_fwd[base : base + 1], 0.0)
    stream1 = stream1 + dot(mid1, proj1)
    value_x, slope_x = gelu_pair(stream1)
    low_x = (value_x * table_live).astype(BF16)
    slope_x = halves(slope_x * table_live)
    taps2 = halves(jnp.concatenate([dot(low_x, weights[4 + k]) for k in range(3)], axis=0))

    hot2 = jnp.concatenate(
        [
            jnp.concatenate([hot_f[0:288], hot_f[64:352], hot_f[128:416]], axis=1),
            jnp.concatenate([hot_r[128:416], hot_r[64:352], hot_r[0:288]], axis=1),
        ],
        axis=0,
    )
    hidden2 = pick(hot2, taps2)
    value2, slope2 = gelu_pair(hidden2)
    live288 = ones_where(code[80:368] > 0.0)
    back2 = dot_nt(grad2_low, proj2) * live288
    own_mask = ones_where(iota((CAP, 1), 0).astype(F32) < own_n)
    mid2 = jnp.concatenate([value2[80:208] * own_mask, value2[368:496] * own_mask], axis=0)
    classes = class_ref[...]
    mid2 = dot(mid2.astype(BF16), classes).astype(BF16)
    own_grad2 = grad2_low[80:208]
    sum2 = dot_tn(mid2, jnp.concatenate([own_grad2, own_grad2], axis=0))

    def to_core(block, total):
        first = jnp.concatenate([total[0:128], total[128:256, 0:B]], axis=1)
        second = jnp.concatenate([total[128:256, B:], total[256:384]], axis=1)
        send0[block] = jnp.where(first_core, second, first).astype(CORE_SUM).reshape(8, 16, 1152)
        acc0[block] = jnp.where(first_core, first, second).reshape(8, 16, 1152)
        push(send0.at[block], recv0.at[block], R0 + block, sibling)

    to_core(1, sum2)
    gh_f = (back2 * slope2[0:288]).astype(BF16)
    gh_r = (back2 * slope2[288:576]).astype(BF16)
    near2 = [
        jnp.concatenate([gh_f[128:288], gh_r[0:160]], axis=0),
        jnp.concatenate([gh_f[64:224], gh_r[64:224]], axis=0),
        jnp.concatenate([gh_f[0:160], gh_r[128:288]], axis=0),
    ]
    active2 = dot_nt(near2[0], weights[4])
    active2 = active2 + dot_nt(near2[1], weights[5])
    active2 = active2 + dot_nt(near2[2], weights[6])
    hot1 = jnp.concatenate([hot_f[128:288], hot_r[128:288]], axis=0)
    around = grad2[64:224]
    grad1 = jnp.concatenate([around, around], axis=0) + active2 * pick(hot1, slope_x)
    grad1_low = grad1.astype(BF16)

    own_low = own_mask.astype(BF16)
    own_hot = jnp.concatenate([hot_f[144:272] * own_low, hot_r[144:272] * own_low], axis=0)
    mid1 = dot(own_hot, dot(mid1, classes).astype(BF16)).astype(BF16)
    sum1 = dot_tn(mid1, jnp.concatenate([grad1_low[16:144], grad1_low[176:304]], axis=0))
    to_core(0, sum1)
    back1 = dot_nt(grad1_low, proj1)
    gh1 = (back1 * pick(hot1, slope1)).astype(BF16)
    near1 = [
        jnp.concatenate([gh1[32:160], gh1[160:288]], axis=0),
        jnp.concatenate([gh1[16:144], gh1[176:304]], axis=0),
        jnp.concatenate([gh1[0:128], gh1[192:320]], axis=0),
    ]

    for block in (1, 0):
        arrive(recv0.at[block], R0 + block)
        for piece in range(8):
            both = acc0[block, piece] + recv0[block, piece].astype(F32)
            px, py = 2 * block + piece // 4, piece % 4
            first = py + other * (px - py)
            second = px + other * (py - px)
            part_f32[first, second] = both
            part_low[first, second] = both.astype(FIRST_SUM)
    for k in (2, 1, 3):
        goal = (two + k) % 4
        push(part_low.at[goal], recv1.at[two], R1 + two, chip(one, goal))

    active1 = dot_nt(near1[0], weights[0])
    active1 = active1 + dot_nt(near1[1], weights[1])
    active1 = active1 + dot_nt(near1[2], weights[2])
    own_code, own_flip = code[160:288], flip[160:288]
    slope_f = jnp.zeros((CAP, C), F32)
    slope_r = jnp.zeros((CAP, C), F32)
    for base in range(4):
        slope_f = jnp.where(own_code == base + 1.0, slope0[base : base + 1], slope_f)
        slope_r = jnp.where(own_flip == base + 1.0, slope0[base : base + 1], slope_r)
    start_f = grad1[16:144] + active1[0:128] * slope_f
    start_r = grad1[176:304] + active1[128:256] * slope_r
    exact = lax.Precision.HIGHEST
    contract = (((1,), (1,)), ((), ()))
    score = lax.dot_general(
        emb_fwd[...], start_f, contract, precision=exact, preferred_element_type=F32
    ) + lax.dot_general(
        emb_rev[...], start_r, contract, precision=exact, preferred_element_type=F32
    )
    score = jnp.where(lane < live_count, score, 0.0) * (1.0 / math.sqrt(C))
    sal_ref[0] = score[0:4]

    for k in (1, 2, 3):
        source = (two + k) % 4
        arrive(recv1.at[source], R1 + source)
    total = part_f32[two]
    for k in (1, 2, 3):
        total = total + recv1[(two + k) % 4].astype(F32)
    part2_f32[...] = total
    part2[...] = total.astype(SECOND_SUM)
    for k in (2, 1, 3):
        goal = (one + k) % 4
        push(part2.at[goal], recv2.at[one], R2 + one, chip(goal, two))
    for k in (1, 2, 3):
        source = (one + k) % 4
        arrive(recv2.at[source], R2 + source)
    total = part2_f32[one]
    for k in (1, 2, 3):
        total = total + recv2[(one + k) % 4].astype(F32)
    for k in range(16):
        part3[k] = total[k : k + 1]
    place = zl * 2 + zh
    for k in (8, 7, 9, 6, 10, 5, 11, 4, 12, 3, 13, 2, 14, 1, 15):
        goal = (z + k) % 16
        push(part3.at[goal % 8 * 2 + goal // 8], recv3.at[place], R3 + place, along_z(goal))
    for k in range(1, 16):
        source = (place + k) % 16
        arrive(recv3.at[source], R3 + source)
    total = part3[place]
    for k in range(1, 16):
        total = total + recv3[(place + k) % 16]
    grad_ref[...] = total * (1.0 / 256.0)

    for copy in started:
        copy.wait_send()


def shards(bases, lengths, cotangent, conv1, proj1, conv2, proj2, embed):
    vmem = pl.BlockSpec(memory_space=pltpu.VMEM)
    saliency, grad = pl.pallas_call(
        kernel,
        out_shape=(
            jax.ShapeDtypeStruct((1, 4, CAP), F32),
            jax.ShapeDtypeStruct((1, 1152), F32),
        ),
        in_specs=[pl.BlockSpec(memory_space=pl.ANY)] * 11,
        out_specs=(vmem, vmem),
        scratch_shapes=[
            pltpu.VMEM((1, CAP), jnp.int32),
            pltpu.SMEM((1, 1), jnp.int32),
            pltpu.VMEM((1, CAP, C), BF16),
            pltpu.VMEM((3, 6, B), BF16),
            pltpu.VMEM((3, C), BF16),
            pltpu.VMEM((3, 6, B), BF16),
            pltpu.VMEM((3, C), BF16),
            pltpu.VMEM((4, C), F32),
            pltpu.VMEM((192, 192), BF16),
            pltpu.VMEM((B, B), BF16),
            pltpu.VMEM((128, 128), F32),
            pltpu.VMEM((24, B), F32),
            pltpu.VMEM((24, B), BF16),
            pltpu.VMEM((8, 24, B), BF16),
            pltpu.VMEM((8, C, B), BF16),
            pltpu.VMEM((80, C), BF16),
            pltpu.VMEM((128, C), BF16),
            pltpu.VMEM((128, C), BF16),
            pltpu.VMEM((8, CAP), F32),
            pltpu.VMEM((6, 8, CAP), F32),
            pltpu.VMEM((8, C), F32),
            pltpu.VMEM((8, C), F32),
            pltpu.VMEM((2, 8, 16, 1152), CORE_SUM),
            pltpu.VMEM((2, 8, 16, 1152), CORE_SUM),
            pltpu.VMEM((2, 8, 16, 1152), F32),
            pltpu.VMEM((4, 4, 16, 1152), F32),
            pltpu.VMEM((4, 4, 16, 1152), FIRST_SUM),
            pltpu.VMEM((4, 4, 16, 1152), FIRST_SUM),
            pltpu.VMEM((4, 16, 1152), SECOND_SUM),
            pltpu.VMEM((4, 16, 1152), SECOND_SUM),
            pltpu.VMEM((4, 16, 1152), F32),
            pltpu.VMEM((16, 1, 1152), F32),
            pltpu.VMEM((16, 1, 1152), F32),
            pltpu.SemaphoreType.DMA((80,)),
            pltpu.SemaphoreType.DMA((80,)),
            pltpu.SemaphoreType.DMA((11,)),
            pltpu.SemaphoreType.REGULAR((4,)),
        ],
        compiler_params=pltpu.CompilerParams(
            collective_id=0, has_side_effects=True, vmem_limit_bytes=60 * 1024 * 1024
        ),
    )(
        bases,
        lengths,
        cotangent,
        conv1,
        proj1,
        conv2,
        proj2,
        embed,
        jnp.asarray(shard_order(), BF16),
        jnp.asarray(class_order(), BF16),
        jnp.asarray(triple_codes(), F32),
    )
    return saliency, grad.reshape(1152)


def solution(mesh):
    in_specs = (
        P("dp", "seq"),
        P("dp", "seq"),
        P("dp", "seq", None),
        P(None, "seq", None),
        P("seq", None),
        P(None, "seq", None),
        P("seq", None),
        P(),
    )
    out_specs = (P("dp", None, "seq"), P(("seq", "dp")))
    return jax.shard_map(shards, mesh=mesh, in_specs=in_specs, out_specs=out_specs, check_vma=False)
```

```python
import math

import jax
import jax.numpy as jnp
import numpy as np
from jax import lax
from jax.experimental import pallas as pl
from jax.experimental.pallas import tpu as pltpu
from jax.sharding import PartitionSpec as P

MESH = pl.DeviceIdType.MESH
F32 = jnp.float32
BF16 = jnp.bfloat16
C = 768
B = 384
CAP = 128
SQRT_HALF = 0.7071067811865476
INV_SQRT_TWO_PI = 0.3989422804014327
CORE_SUM = BF16
FIRST_SUM = BF16
SECOND_SUM = BF16
FAR = 1.0e6


def shard_order():
    table = np.zeros((192, 192), np.float32)
    for row in range(192):
        piece, within = divmod(row, 48)
        if piece < 3:
            source = within // 6 * 24 + piece * 6 + within % 6
        else:
            half, rest = divmod(within, 24)
            source = rest // 3 * 24 + 18 + half * 3 + rest % 3
        table[row, source] = 1.0
    return table


def class_order():
    table = np.zeros((B, B), np.float32)
    for row in range(B):
        table[row, row % 3 * 128 + row // 3] = 1.0
    return table


def triple_codes():
    table = np.zeros((128, 128), np.float32)
    for row in range(125):
        table[row, :3] = row // 25, row // 5 % 5, row % 5
    return table


def gelu_pair(values):
    bell = 1.0 + lax.erf(values * SQRT_HALF)
    slope = 0.5 * bell + values * jnp.exp(-0.5 * values * values) * INV_SQRT_TWO_PI
    return 0.5 * values * bell, slope


def dot(left, right):
    return jnp.dot(left, right, preferred_element_type=F32)


def dot_nt(left, right):
    return lax.dot_general(left, right, (((1,), (1,)), ((), ())), preferred_element_type=F32)


def dot_tn(left, right):
    return lax.dot_general(left, right, (((0,), (0,)), ((), ())), preferred_element_type=F32)


def halves(values):
    high = values.astype(BF16)
    return high, (values - high.astype(F32)).astype(BF16)


def pick(onehot, pair):
    return dot(onehot, pair[0]) + dot(onehot, pair[1])


def ones_where(mask):
    return jnp.where(mask, 1.0, 0.0)


def iota(shape, dim):
    return lax.broadcasted_iota(jnp.int32, shape, dim)


def kernel(
    bases_hbm,
    len_hbm,
    cot_hbm,
    conv1_hbm,
    proj1_hbm,
    conv2_hbm,
    proj2_hbm,
    embed_hbm,
    order_hbm,
    class_hbm,
    codes_hbm,
    sal_ref,
    grad_ref,
    bases_ref,
    len_ref,
    cot_ref,
    conv1_ref,
    proj1_ref,
    conv2_ref,
    proj2_ref,
    embed_ref,
    order_ref,
    class_ref,
    codes_ref,
    pack32,
    shard,
    zbuf,
    weights,
    tail,
    left_rows,
    right_rows,
    enc_own,
    enc_all,
    emb_fwd,
    emb_rev,
    send0,
    recv0,
    acc0,
    part_f32,
    part_low,
    recv1,
    part2,
    recv2,
    part2_f32,
    part3,
    recv3,
    send_sem,
    recv_sem,
    copy_sem,
    known_sem,
):
    seq = lax.axis_index("seq")
    dpi = lax.axis_index("dp")
    x, y, zl = seq // 32, seq // 8 % 4, seq % 8
    zh, core = dpi // 2, dpi % 2
    z = zh * 8 + zl
    other = 1 - core
    one = y + core * (x - y)
    two = x + core * (y - x)

    def chip(first, second):
        cx = second + core * (first - second)
        cy = first + core * (second - first)
        return ((cx * 4 + cy) * 8 + zl, dpi)

    def along_z(target):
        return ((x * 4 + y) * 8 + target % 8, target // 8 * 2 + core)

    def along_seq(offset):
        return ((seq + offset + 128) % 128, dpi)

    sibling = (seq, zh * 2 + other)

    barrier = pltpu.get_barrier_semaphore()
    line_x = [(((x + k) % 4 * 4 + y) * 8 + zl, dpi) for k in (1, 3)]
    line_y = [((x * 4 + (y + k) % 4) * 8 + zl, dpi) for k in (1, 3)]
    near_z = [along_z((z + k) % 16) for k in (2, 14)]
    far_z = [along_z((z + k) % 16) for k in (4, 12)]
    partners = [sibling] + line_x + line_y + near_z
    partners += [along_z((z + k) % 16) for k in (1, 15)]
    for device in partners:
        pl.semaphore_signal(barrier, inc=1, device_id=device, device_id_type=MESH)

    loads = []
    for k, (source, target) in enumerate(
        (
            (conv1_hbm, conv1_ref),
            (conv2_hbm, conv2_ref),
            (proj1_hbm, proj1_ref),
            (proj2_hbm, proj2_ref),
            (len_hbm, len_ref),
            (bases_hbm, bases_ref),
            (embed_hbm, embed_ref),
            (cot_hbm, cot_ref),
            (order_hbm, order_ref),
            (class_hbm, class_ref),
            (codes_hbm, codes_ref),
        )
    ):
        copy = pltpu.make_async_copy(source, target, copy_sem.at[k])
        copy.start()
        loads.append(copy)

    def announce(devices, slot):
        for device in devices:
            pl.semaphore_signal(
                known_sem.at[slot], inc=1, device_id=device, device_id_type=MESH
            )

    def heard(slot):
        pl.semaphore_wait(known_sem.at[slot], 2)

    used = {"send": 0}
    started = []

    def push(source, target, slot, device):
        copy = pltpu.make_async_remote_copy(
            src_ref=source,
            dst_ref=target,
            send_sem=send_sem.at[used["send"]],
            recv_sem=recv_sem.at[slot],
            device_id=device,
            device_id_type=MESH,
        )
        used["send"] += 1
        copy.start()
        started.append(copy)

    def arrive(target, slot):
        pltpu.make_async_remote_copy(
            src_ref=target,
            dst_ref=target,
            send_sem=send_sem.at[0],
            recv_sem=recv_sem.at[slot],
            device_id=sibling,
            device_id_type=MESH,
        ).wait_recv()

    for copy in loads:
        copy.wait()
    lane = iota((1, CAP), 1)
    live_count = len_ref[0, 0]
    code_row = jnp.where(lane < live_count, bases_ref[...] + 1, 0).astype(F32)
    enc_own[...] = jnp.broadcast_to(code_row, (8, CAP))
    own_cot = cot_ref[0]
    choose = iota((80, CAP), 1) - iota((80, CAP), 0) == live_count - 80
    tail[...] = dot(ones_where(choose).astype(BF16), own_cot).astype(BF16)
    left_rows[96:128] = jnp.zeros((32, C), BF16)
    right_rows[96:128] = jnp.zeros((32, C), BF16)
    first_core = core == 0
    for k in range(3):
        pack32[6 * k : 6 * k + 6] = jnp.where(
            first_core, conv1_ref[k].astype(F32), conv2_ref[k].astype(F32)
        )
    proj_rows = jnp.where(first_core, proj1_ref[...].astype(F32), proj2_ref[...].astype(F32))
    pack32[18:21] = proj_rows[:, :B]
    pack32[21:24] = proj_rows[:, B:]
    shard[...] = pack32[...].astype(BF16)
    zbuf[zl] = pack32[...].astype(BF16)
    emb_fwd[0:4] = embed_ref[...]
    emb_fwd[4:8] = jnp.zeros((4, C), F32)
    emb_rev[4:8] = jnp.zeros((4, C), F32)
    for k in range(4):
        emb_rev[k : k + 1] = embed_ref[3 - k : 4 - k]

    pl.semaphore_wait(barrier, len(partners))

    Z, D1F, D1H, D2F, D2H, SIB, HALO, ENC, R0, R1, R2, R3 = (
        0, 8, 10, 12, 20, 28, 44, 48, 54, 56, 60, 64,
    )
    turn_z = 1 - 2 * core

    def z_at(offset):
        return along_z((z + offset * turn_z + 16) % 16)

    def z_slot(offset):
        return (zl + offset * turn_z + 8) % 8

    def z_wait(offset):
        arrive(zbuf.at[z_slot(offset)], Z + z_slot(offset))

    def z_pass(offset, onward):
        z_wait(offset)
        held = zbuf.at[z_slot(offset)]
        push(held, held, Z + z_slot(offset), z_at(onward))

    for offset in (2, -2, 1, -1):
        push(shard, zbuf.at[zl], Z + zl, z_at(offset))
    announce(near_z, 0)
    z_pass(-1, 2)
    z_pass(1, -2)
    z_pass(-2, 2)
    heard(0)
    announce(far_z, 1)
    for offset in (2, 3, -3, -4):
        z_wait(offset)

    def block_of(owner, first, second, piece, count):
        group = first * (1 + 3 * owner) + second * (4 - 3 * owner)
        rows = pl.ds(pl.multiple_of(group * 48, 16), 48)
        return weights.at[pl.ds(4 * owner + piece, count), rows, :]

    gathered = zbuf[...].astype(F32).reshape(192, B).astype(BF16)
    moved = dot(order_ref[...], gathered).astype(BF16)
    own_rows = pl.ds(pl.multiple_of((x * 4 + y) * 48, 16), 48)
    for k in range(4):
        weights[4 * core + k, own_rows, :] = moved[48 * k : 48 * k + 48]

    steps = (0, 3, 1, 2)

    def line(step, turn, piece=0, count=4):
        return block_of(core, (one + steps[step]) % 4, (two + steps[turn]) % 4, piece, count)

    one_up, one_down = chip((one + 1) % 4, two), chip((one + 3) % 4, two)
    two_up, two_down = chip(one, (two + 1) % 4), chip(one, (two + 3) % 4)

    def to_sibling(step, turn):
        push(line(step, turn), line(step, turn), SIB + step * 4 + turn, sibling)

    def to_second(step):
        push(line(step, 0), line(step, 0), D2F + step * 2, two_up)
        push(line(step, 0), line(step, 0), D2F + step * 2 + 1, two_down)

    def relay_second(step):
        arrive(line(step, 1), D2F + step * 2)
        push(line(step, 1, 0, 2), line(step, 1, 0, 2), D2H + step * 2, two_up)
        to_sibling(step, 1)
        arrive(line(step, 2), D2F + step * 2 + 1)
        push(line(step, 2, 2, 2), line(step, 2, 2, 2), D2H + step * 2 + 1, two_down)
        to_sibling(step, 2)

    push(line(0, 0), line(0, 0), D1F, one_up)
    push(line(0, 0), line(0, 0), D1F + 1, one_down)
    to_second(0)
    to_sibling(0, 0)
    heard(1)
    announce(line_x, 2)
    arrive(line(1, 0), D1F)
    push(line(1, 0, 0, 2), line(1, 0, 0, 2), D1H, one_up)
    to_second(1)
    to_sibling(1, 0)
    heard(2)
    announce(line_y, 3)
    arrive(line(2, 0), D1F + 1)
    push(line(2, 0, 2, 2), line(2, 0, 2, 2), D1H + 1, one_down)
    to_second(2)
    to_sibling(2, 0)
    heard(3)
    for k in (1, 2, 3):
        push(enc_own, enc_all.at[k - 1], ENC + k - 1, along_seq(k))
        push(enc_own, enc_all.at[2 + k], ENC + 2 + k, along_seq(-k))
    push(tail, left_rows.at[0:80], HALO, along_seq(1))
    push(cot_ref.at[0, 0:80], right_rows.at[0:80], HALO + 1, along_seq(-1))
    push(tail.at[64:80], left_rows.at[80:96], HALO + 2, along_seq(2))
    push(cot_ref.at[0, 0:16], right_rows.at[80:96], HALO + 3, along_seq(-2))
    relay_second(0)
    arrive(line(3, 0, 0, 2), D1H)
    arrive(line(3, 0, 2, 2), D1H + 1)
    to_second(3)
    to_sibling(3, 0)
    for step in (1, 2, 3):
        relay_second(step)
    for step in range(4):
        arrive(line(step, 3, 0, 2), D2H + step * 2)
        arrive(line(step, 3, 2, 2), D2H + step * 2 + 1)
        to_sibling(step, 3)

    for k in range(6):
        arrive(enc_all.at[k], ENC + k)
    own_n = jnp.sum(ones_where(code_row > 0.0), axis=1, keepdims=True)
    lane_f = lane.astype(F32)
    rows_t = (iota((448, 1), 0) - 160).astype(F32)
    pieces = [(code_row, jnp.zeros((1, 1), F32))]
    left_n, right_n = [], []
    left_at, right_at = jnp.zeros((1, 1), F32), own_n
    for k in (1, 2, 3):
        there = jnp.where(seq >= k, 1.0, 0.0)
        row = enc_all[k - 1, 0:1] * there
        count = jnp.sum(ones_where(row > 0.0), axis=1, keepdims=True)
        left_at = left_at - count
        left_n.append(count)
        pieces.append((row, left_at))
        there = jnp.where(seq + k <= 127, 1.0, 0.0)
        row = enc_all[2 + k, 0:1] * there
        count = jnp.sum(ones_where(row > 0.0), axis=1, keepdims=True)
        pieces.append((row, right_at))
        right_at = right_at + count
        right_n.append(count)
    found = jnp.zeros((448, CAP), F32)
    for row, start in pieces:
        found = found + jnp.where(rows_t == lane_f + start, row, 0.0)
    code = jnp.sum(found, axis=1, keepdims=True)
    flip = jnp.where(code > 0.0, 5.0 - code, 0.0)
    triple_f = 25.0 * code[0:416] + 5.0 * code[16:432] + code[32:448]
    triple_r = 25.0 * flip[32:448] + 5.0 * flip[16:432] + flip[0:416]
    hot_f = ones_where(triple_f == lane_f).astype(BF16)
    hot_r = ones_where(triple_r == lane_f).astype(BF16)

    arrive(left_rows.at[0:80], HALO)
    arrive(right_rows.at[0:80], HALO + 1)
    arrive(left_rows.at[80:96], HALO + 2)
    arrive(right_rows.at[80:96], HALO + 3)
    t288 = (iota((288, 1), 0) - 80).astype(F32)
    own_pos = jnp.where(lane_f < own_n, lane_f, FAR)
    left_pos = jnp.where(lane_f >= 80.0 - left_n[0], lane_f - 80.0, FAR)
    left_far = jnp.where(left_n[1] > 0.0, lane_f - 96.0 - left_n[0], FAR)
    left_pos = jnp.where(lane_f < 80.0, left_pos, jnp.where(lane_f < 96.0, left_far, FAR))
    right_pos = jnp.where(lane_f < right_n[0], lane_f + own_n, FAR)
    right_far = jnp.where(right_n[1] > 0.0, lane_f - 80.0 + own_n + right_n[0], FAR)
    right_pos = jnp.where(lane_f < 80.0, right_pos, jnp.where(lane_f < 96.0, right_far, FAR))
    cot = (
        dot(ones_where(t288 == own_pos).astype(BF16), own_cot)
        + dot(ones_where(t288 == left_pos).astype(BF16), left_rows[...])
        + dot(ones_where(t288 == right_pos).astype(BF16), right_rows[...])
    )
    grad2 = 0.5 * cot
    grad2_low = grad2.astype(BF16)

    for step in range(4):
        for turn in range(4):
            theirs = block_of(
                other,
                (x + core * (y - x) + steps[step]) % 4,
                (y + core * (x - y) + steps[turn]) % 4,
                0,
                4,
            )
            arrive(theirs, SIB + step * 4 + turn)

    def projection(block):
        rows = weights[4 * block + 3].astype(F32).reshape(16, 2, 24, B)
        return [rows[:, half].reshape(B, B).astype(BF16) for half in range(2)]

    proj1 = jnp.concatenate(projection(0), axis=1)
    proj2 = jnp.concatenate(projection(1), axis=1)

    before_code, mid_code, after_code = codes_ref[:, 0:1], codes_ref[:, 1:2], codes_ref[:, 2:3]
    value0, slope0 = gelu_pair(emb_fwd[...])
    low0 = value0.astype(BF16)
    hidden1 = jnp.zeros((128, B), F32)
    for k, column in enumerate((before_code, mid_code, after_code)):
        rows = dot(low0, weights[k])
        for base in range(4):
            hidden1 = hidden1 + jnp.where(column == base + 1.0, rows[base : base + 1], 0.0)
    table_live = ones_where(mid_code > 0.0)
    hidden1 = hidden1 * table_live
    value1, slope1 = gelu_pair(hidden1)
    mid1 = value1.astype(BF16)
    slope1 = halves(slope1 * table_live)
    stream1 = jnp.zeros((128, C), F32)
    for base in range(4):
        stream1 = stream1 + jnp.where(mid_code == base + 1.0, emb_fwd[base : base + 1], 0.0)
    stream1 = stream1 + dot(mid1, proj1)
    value_x, slope_x = gelu_pair(stream1)
    low_x = (value_x * table_live).astype(BF16)
    slope_x = halves(slope_x * table_live)
    taps2 = halves(jnp.concatenate([dot(low_x, weights[4 + k]) for k in range(3)], axis=0))

    hot2 = jnp.concatenate(
        [
            jnp.concatenate([hot_f[0:288], hot_f[64:352], hot_f[128:416]], axis=1),
            jnp.concatenate([hot_r[128:416], hot_r[64:352], hot_r[0:288]], axis=1),
        ],
        axis=0,
    )
    hidden2 = pick(hot2, taps2)
    value2, slope2 = gelu_pair(hidden2)
    live288 = ones_where(code[80:368] > 0.0)
    back2 = dot_nt(grad2_low, proj2) * live288
    own_mask = ones_where(iota((CAP, 1), 0).astype(F32) < own_n)
    mid2 = jnp.concatenate([value2[80:208] * own_mask, value2[368:496] * own_mask], axis=0)
    classes = class_ref[...]
    mid2 = dot(mid2.astype(BF16), classes).astype(BF16)
    own_grad2 = grad2_low[80:208]
    sum2 = dot_tn(mid2, jnp.concatenate([own_grad2, own_grad2], axis=0))

    def to_core(block, total):
        first = jnp.concatenate([total[0:128], total[128:256, 0:B]], axis=1)
        second = jnp.concatenate([total[128:256, B:], total[256:384]], axis=1)
        send0[block] = jnp.where(first_core, second, first).astype(CORE_SUM).reshape(8, 16, 1152)
        acc0[block] = jnp.where(first_core, first, second).reshape(8, 16, 1152)
        push(send0.at[block], recv0.at[block], R0 + block, sibling)

    to_core(1, sum2)
    gh_f = (back2 * slope2[0:288]).astype(BF16)
    gh_r = (back2 * slope2[288:576]).astype(BF16)
    near2 = [
        jnp.concatenate([gh_f[128:288], gh_r[0:160]], axis=0),
        jnp.concatenate([gh_f[64:224], gh_r[64:224]], axis=0),
        jnp.concatenate([gh_f[0:160], gh_r[128:288]], axis=0),
    ]
    active2 = dot_nt(near2[0], weights[4])
    active2 = active2 + dot_nt(near2[1], weights[5])
    active2 = active2 + dot_nt(near2[2], weights[6])
    hot1 = jnp.concatenate([hot_f[128:288], hot_r[128:288]], axis=0)
    around = grad2[64:224]
    grad1 = jnp.concatenate([around, around], axis=0) + active2 * pick(hot1, slope_x)
    grad1_low = grad1.astype(BF16)

    own_low = own_mask.astype(BF16)
    own_hot = jnp.concatenate([hot_f[144:272] * own_low, hot_r[144:272] * own_low], axis=0)
    mid1 = dot(own_hot, dot(mid1, classes).astype(BF16)).astype(BF16)
    sum1 = dot_tn(mid1, jnp.concatenate([grad1_low[16:144], grad1_low[176:304]], axis=0))
    to_core(0, sum1)

    for block in (1, 0):
        arrive(recv0.at[block], R0 + block)
        for piece in range(8):
            both = acc0[block, piece] + recv0[block, piece].astype(F32)
            px, py = 2 * block + piece // 4, piece % 4
            first = py + other * (px - py)
            second = px + other * (py - px)
            part_f32[first, second] = both
            part_low[first, second] = both.astype(FIRST_SUM)
    for k in (2, 1, 3):
        goal = (two + k) % 4
        push(part_low.at[goal], recv1.at[two], R1 + two, chip(one, goal))

    back1 = dot_nt(grad1_low, proj1)
    gh1 = (back1 * pick(hot1, slope1)).astype(BF16)
    near1 = [
        jnp.concatenate([gh1[32:160], gh1[160:288]], axis=0),
        jnp.concatenate([gh1[16:144], gh1[176:304]], axis=0),
        jnp.concatenate([gh1[0:128], gh1[192:320]], axis=0),
    ]
    active1 = dot_nt(near1[0], weights[0])
    active1 = active1 + dot_nt(near1[1], weights[1])
    active1 = active1 + dot_nt(near1[2], weights[2])
    own_code, own_flip = code[160:288], flip[160:288]
    slope_f = jnp.zeros((CAP, C), F32)
    slope_r = jnp.zeros((CAP, C), F32)
    for base in range(4):
        slope_f = jnp.where(own_code == base + 1.0, slope0[base : base + 1], slope_f)
        slope_r = jnp.where(own_flip == base + 1.0, slope0[base : base + 1], slope_r)
    start_f = grad1[16:144] + active1[0:128] * slope_f
    start_r = grad1[176:304] + active1[128:256] * slope_r
    exact = lax.Precision.HIGHEST
    contract = (((1,), (1,)), ((), ()))
    score = lax.dot_general(
        emb_fwd[...], start_f, contract, precision=exact, preferred_element_type=F32
    ) + lax.dot_general(
        emb_rev[...], start_r, contract, precision=exact, preferred_element_type=F32
    )
    score = jnp.where(lane < live_count, score, 0.0) * (1.0 / math.sqrt(C))
    sal_ref[0] = score[0:4]

    for k in (1, 2, 3):
        source = (two + k) % 4
        arrive(recv1.at[source], R1 + source)
    total = part_f32[two]
    for k in (1, 2, 3):
        total = total + recv1[(two + k) % 4].astype(F32)
    part2_f32[...] = total
    part2[...] = total.astype(SECOND_SUM)
    for k in (2, 1, 3):
        goal = (one + k) % 4
        push(part2.at[goal], recv2.at[one], R2 + one, chip(goal, two))
    for k in (1, 2, 3):
        source = (one + k) % 4
        arrive(recv2.at[source], R2 + source)
    total = part2_f32[one]
    for k in (1, 2, 3):
        total = total + recv2[(one + k) % 4].astype(F32)
    for k in range(16):
        part3[k] = total[k : k + 1]
    place = zl * 2 + zh
    for k in (8, 7, 9, 6, 10, 5, 11, 4, 12, 3, 13, 2, 14, 1, 15):
        goal = (z + k) % 16
        push(part3.at[goal % 8 * 2 + goal // 8], recv3.at[place], R3 + place, along_z(goal))
    for k in range(1, 16):
        source = (place + k) % 16
        arrive(recv3.at[source], R3 + source)
    total = part3[place]
    for k in range(1, 16):
        total = total + recv3[(place + k) % 16]
    grad_ref[...] = total * (1.0 / 256.0)

    for copy in started:
        copy.wait_send()


def shards(bases, lengths, cotangent, conv1, proj1, conv2, proj2, embed):
    vmem = pl.BlockSpec(memory_space=pltpu.VMEM)
    saliency, grad = pl.pallas_call(
        kernel,
        out_shape=(
            jax.ShapeDtypeStruct((1, 4, CAP), F32),
            jax.ShapeDtypeStruct((1, 1152), F32),
        ),
        in_specs=[pl.BlockSpec(memory_space=pl.ANY)] * 11,
        out_specs=(vmem, vmem),
        scratch_shapes=[
            pltpu.VMEM((1, CAP), jnp.int32),
            pltpu.SMEM((1, 1), jnp.int32),
            pltpu.VMEM((1, CAP, C), BF16),
            pltpu.VMEM((3, 6, B), BF16),
            pltpu.VMEM((3, C), BF16),
            pltpu.VMEM((3, 6, B), BF16),
            pltpu.VMEM((3, C), BF16),
            pltpu.VMEM((4, C), F32),
            pltpu.VMEM((192, 192), BF16),
            pltpu.VMEM((B, B), BF16),
            pltpu.VMEM((128, 128), F32),
            pltpu.VMEM((24, B), F32),
            pltpu.VMEM((24, B), BF16),
            pltpu.VMEM((8, 24, B), BF16),
            pltpu.VMEM((8, C, B), BF16),
            pltpu.VMEM((80, C), BF16),
            pltpu.VMEM((128, C), BF16),
            pltpu.VMEM((128, C), BF16),
            pltpu.VMEM((8, CAP), F32),
            pltpu.VMEM((6, 8, CAP), F32),
            pltpu.VMEM((8, C), F32),
            pltpu.VMEM((8, C), F32),
            pltpu.VMEM((2, 8, 16, 1152), CORE_SUM),
            pltpu.VMEM((2, 8, 16, 1152), CORE_SUM),
            pltpu.VMEM((2, 8, 16, 1152), F32),
            pltpu.VMEM((4, 4, 16, 1152), F32),
            pltpu.VMEM((4, 4, 16, 1152), FIRST_SUM),
            pltpu.VMEM((4, 4, 16, 1152), FIRST_SUM),
            pltpu.VMEM((4, 16, 1152), SECOND_SUM),
            pltpu.VMEM((4, 16, 1152), SECOND_SUM),
            pltpu.VMEM((4, 16, 1152), F32),
            pltpu.VMEM((16, 1, 1152), F32),
            pltpu.VMEM((16, 1, 1152), F32),
            pltpu.SemaphoreType.DMA((80,)),
            pltpu.SemaphoreType.DMA((80,)),
            pltpu.SemaphoreType.DMA((11,)),
            pltpu.SemaphoreType.REGULAR((4,)),
        ],
        compiler_params=pltpu.CompilerParams(
            collective_id=0, has_side_effects=True, vmem_limit_bytes=60 * 1024 * 1024
        ),
    )(
        bases,
        lengths,
        cotangent,
        conv1,
        proj1,
        conv2,
        proj2,
        embed,
        jnp.asarray(shard_order(), BF16),
        jnp.asarray(class_order(), BF16),
        jnp.asarray(triple_codes(), F32),
    )
    return saliency, grad.reshape(1152)


def solution(mesh):
    in_specs = (
        P("dp", "seq"),
        P("dp", "seq"),
        P("dp", "seq", None),
        P(None, "seq", None),
        P("seq", None),
        P(None, "seq", None),
        P("seq", None),
        P(),
    )
    out_specs = (P("dp", None, "seq"), P(("seq", "dp")))
    return jax.shard_map(shards, mesh=mesh, in_specs=in_specs, out_specs=out_specs, check_vma=False)
```
